32 devices in a mesh: band: 4 (over y, x), tm: 8 (over z, core).
Axes of the slice: x: 2, y: 2, z: 4, core: 2. Of those that a mesh axis runs over, the one named last changes fastest.
Arguments:
- timeline: bfloat16 [4096, 1024], P('tm', 'band'), parts along dimension 1, may hold values from -6 to 6
- pointing: int32 [4096, 1024], P('tm', 'band'), parts along dimension 1, may hold values from 0 to 127
- plate_angle: float32 [4096], P('tm'), may hold values from -3.140625 to 3.140625
- detector_angle: float32 [1024], P('band'), parts along dimension 0, may hold values from -3.140625 to 3.140625
- detector_weight: float32 [1024], P('band'), parts along dimension 0, may hold values from 0.3 to 3
- kernel: bfloat16 [4100], P('band'), parts along dimension 0, may hold values from -0.1875 to 0.1875
- tile_owner: int32 [512, 4], P('tm', 'band'), parts along dimension 1, may hold values from 0 to 7; in each aligned block of 64 rows (0 to 63, 64 to 127, ...) at most 16 rows name the same one
- tile_block: int32 [512, 4], P('tm', 'band'), parts along dimension 1, may hold values from 0 to 8191
- wiener: float32 [12, 4096, 2048], P('band', 'tm'), parts along dimension 0, may hold values from 0.05 to 1
Outputs:
- filtered_spectrum: float32 [2, 12, 4096, 2048], P(None, 'band', 'tm'), parts along dimension 1
The draws below stay inside these ranges and needn't reach their ends.
There are 4 independent parts, one for each index of `band`. The reference program is written for one: setup_inputs(seed, part) draws one part's arguments, and reference() takes and returns one part's arrays. A program takes and returns all parts, laid end to end along the dimension named above; an argument that names none is the same for every part. Nothing has to cross between parts.
Inputs may be any that keep to these rules, and one draw needn't show every extreme that they name: `tile_owner`: at most 16 of the 64 tiles of one time shard name the same owner, some shard's tiles name one owner exactly 16 times, and every owner is named by some tile.
All inputs are finite; a program needn't handle non-finite values.
Results may differ from the reference program's by a relative error of at most 0.0029.
Values may be sent and summed in bfloat16 or wider, within the bound.
No kernel may reach another device: no remote copies, remote signals or barrier semaphores. Data moves between devices by JAX's collectives and lax.ppermute only.
A program may use at most 192 MiB of HBM per device.

```python
import math
import jax
import jax.numpy as jnp
import numpy as np
from jax import lax

DET = 256
HALF = 512
PIECE = 16
DGRP = 128
BPIX = 128
ROWS = 2048
COLS = 4096
SAMPLES = 4096
KLEN = 1025
NTILE = 64
TILES = 512
CAP = 16
ROWS_OWN = 256
COL_BLOCKS = 32
OWNBLK = 8192
N_TM = 8


def set_ends(entries, own_key, least, largest):
    longest = entries.shape.index(max(entries.shape))
    spots = []
    for shift in (0, 1):
        where = [jax.random.randint(jax.random.fold_in(own_key, axis), (), 0, length) for axis, length in enumerate(entries.shape)]
        where[longest] = (where[longest] + shift) % entries.shape[longest]
        spots.append(tuple(where))
    return entries.at[spots[0]].set(least).at[spots[1]].set(largest)


def block_levels(rng, dims, split, least, top_value):
    level = 1.0
    for position, blocks in split:
        draws = jax.random.uniform(jax.random.fold_in(jax.random.fold_in(rng, 6), position), (blocks,), jnp.float32, least / len(split), top_value / len(split))
        level = level * jnp.repeat(jnp.exp(draws), dims[position] // blocks).reshape((-1,) + (1,) * (len(dims) - 1 - position))
    return level


def routed_block(stream_key, own, number, rows, count, top, reach, lean):
    sequence = jax.random.permutation(stream_key, count)
    crowded, ordinary = shares(count, rows * top, reach, lean, True), shares(count, rows * top, reach, lean, False)
    places = jnp.arange(count)

    def named(lengths, offset_by):
        used = int((lengths > 0).sum())
        fixed = max(1, used // 4)
        passed = fixed + (places - fixed + offset_by * (used - fixed)) % max(1, count - fixed)
        return jnp.zeros((count,), jnp.int32).at[sequence[jnp.where(places < fixed, places, passed)]].set(jnp.asarray(lengths, jnp.int32))

    lengths = jnp.where(number % 4 == 0, named(crowded, number // 4), named(ordinary, number - number // 4 - 1))
    mixed = jax.random.permutation(jax.random.fold_in(own, 3), count)
    donor, taker = mixed[0:count // 2 * 2:2], mixed[1:count // 2 * 2:2]
    room = jnp.minimum(lengths[donor] - 1, reach - lengths[taker]) // 2
    room = jnp.where((donor == sequence[0]) | (taker == sequence[0]) | (lengths[taker] == 0), 0, jnp.maximum(room, 0))
    passed = jax.random.randint(jax.random.fold_in(own, 4), (count // 2,), 0, 1 << 20) % (room + 1)
    lengths = lengths.at[donor].add(-passed).at[taker].add(passed)
    items = jnp.searchsorted(jnp.cumsum(lengths), jnp.arange(rows * top), side="right").astype(jnp.int32)
    grid = items.reshape(top, rows).T
    grid = grid[jax.random.permutation(jax.random.fold_in(own, 1), rows)]
    offset_by = jax.random.randint(jax.random.fold_in(own, 2), (rows, 1), 0, top)
    return jnp.take_along_axis(grid, (jnp.arange(top)[None, :] + offset_by) % top, axis=1)


def shares(count, total, reach, slope, full):
    weights = [(1 << 20) // math.isqrt(standing ** slope) + 1 for standing in range(1, count + 1)]
    largest = reach if full else min(reach, max(-(-total // count), total * weights[0] // sum(weights)))
    least = 1 if total - largest >= count - 1 else 0
    holding, surplus = [largest] + [least] * (count - 1), total - largest - least * (count - 1)
    while surplus > 0:
        free = [i for i in range(1, count) if holding[i] < largest] or [i for i in range(1, count) if holding[i] < reach]
        whole, budget = sum([weights[i] for i in free]), surplus
        for i in free:
            addition = min(reach - holding[i], max(1, budget * weights[i] // whole), surplus)
            holding[i] = holding[i] + addition
            surplus = surplus - addition
    return np.array(holding)


def scatter_about(key, dims, width, most, pieces=(), kind=jnp.bfloat16):
    entries = width * jax.random.normal(key, dims, jnp.float32)
    if pieces:
        entries = entries * block_levels(key, dims, pieces, -0.22, 0.18)
    return jnp.clip(entries, -most, most).astype(kind)


def setup_inputs(seed: int = 0, part: int = 0) -> dict:
    key_list = jax.random.split(jax.random.key(seed), 10)
    part_keys = jax.random.split(jax.random.fold_in(key_list[9], part), 10)
    timeline = scatter_about(part_keys[0], (SAMPLES, DET), 1.0, 6.0, ((0, 8),))
    pointing = set_ends(jax.random.randint(part_keys[1], (SAMPLES, DET), 0, BPIX), jax.random.fold_in(part_keys[1], 1), 0, BPIX - 1).astype(jnp.int32)
    plate_angle = jnp.clip(jax.random.uniform(key_list[2], (SAMPLES,), jnp.float32, -3.140625, 3.140625), -3.140625, 3.140625)
    detector_angle = jnp.clip(jax.random.uniform(part_keys[3], (DET,), jnp.float32, -3.140625, 3.140625), -3.140625, 3.140625)
    detector_weight = jnp.clip(jnp.exp(jax.random.uniform(part_keys[4], (DET,), jnp.float32, math.log(0.3), math.log(3.0))), 0.3, 3.0)
    kernel = scatter_about(part_keys[5], (KLEN,), KLEN ** -0.5, 0.1875)
    tile_owner_keys = jax.random.split(jax.random.fold_in(part_keys[6], 1), TILES // NTILE)
    tile_owner_turns = jax.random.permutation(jax.random.fold_in(part_keys[6], 3), TILES // NTILE)
    tile_owner = jax.vmap(lambda own, number: routed_block(jax.random.fold_in(part_keys[6], 2), own, number, NTILE, N_TM, 1, CAP, 2))(tile_owner_keys, tile_owner_turns).reshape((TILES, 1))
    tile_block = set_ends(jax.random.randint(part_keys[7], (TILES, 1), 0, OWNBLK), jax.random.fold_in(part_keys[7], 1), 0, OWNBLK - 1).astype(jnp.int32)
    wiener = jnp.clip(0.05 + 0.95 * jax.random.uniform(part_keys[8], (3, COLS, ROWS), jnp.float32) ** block_levels(part_keys[8], (3, COLS, ROWS), ((1, 8),), -0.2, 0.2), 0.05, 1.0)
    return {"timeline": timeline, "pointing": pointing, "plate_angle": plate_angle, "detector_angle": detector_angle, "detector_weight": detector_weight, "kernel": kernel, "tile_owner": tile_owner, "tile_block": tile_block, "wiener": wiener}


def band_matrix(kernel):
    half_width = (kernel.shape[0] - 1) // 2
    pattern = jnp.concatenate([kernel, jnp.zeros((half_width,), kernel.dtype)])
    repeated = jnp.tile(pattern, half_width)[: 3 * half_width * half_width]
    return repeated.reshape(half_width, 3 * half_width)


def apply_band(padded, band_rows):
    half_width = band_rows.shape[0]
    blocks = padded.reshape(-1, half_width, padded.shape[1])
    windows = jnp.concatenate([blocks[:-2], blocks[1:-1], blocks[2:]], axis=1)
    result = jnp.einsum("ij,bjc->bic", band_rows.astype(jnp.float32), windows.astype(jnp.float32), precision=lax.Precision.HIGHEST)
    return result.reshape(-1, padded.shape[1])


def reference(timeline, pointing, plate_angle, detector_angle, detector_weight, kernel, tile_owner, tile_block, wiener):
    band_rows = band_matrix(kernel)
    padded = jnp.pad(timeline, ((HALF, HALF), (0, 0)))
    weighted = detector_weight[None, :] * apply_band(padded, band_rows)
    angle = 2.0 * plate_angle[:, None] + detector_angle[None, :]
    stokes = jnp.stack([weighted, weighted * jnp.cos(2.0 * angle), weighted * jnp.sin(2.0 * angle)]).astype(jnp.bfloat16)
    sample_tile = (jnp.arange(SAMPLES, dtype=jnp.int32) // PIECE)[:, None] * (DET // DGRP) + (jnp.arange(DET, dtype=jnp.int32) // DGRP)[None, :]
    owners = tile_owner[:, 0][sample_tile]
    blocks = tile_block[:, 0][sample_tile]
    map_row = owners * ROWS_OWN + blocks // COL_BLOCKS
    map_col = (blocks % COL_BLOCKS) * BPIX + pointing
    flat = (map_row * COLS + map_col).reshape(-1).astype(jnp.int32)
    sums = jax.ops.segment_sum(stokes.reshape(3, -1).T.astype(jnp.float32), flat, num_segments=ROWS * COLS)
    sky = sums.T.reshape(3, ROWS, COLS)
    spectrum = jnp.fft.fft2(sky, norm="ortho")
    real_part = jnp.real(spectrum).astype(jnp.float32)
    imag_part = jnp.imag(spectrum).astype(jnp.float32)
    stacked = jnp.stack([real_part, imag_part]).transpose(0, 1, 3, 2)
    return stacked * wiener[None]
```

```python
import functools
import math

import jax
import jax.numpy as jnp
from jax import lax
from jax.experimental import pallas as pl
from jax.experimental.pallas import tpu as pltpu
from jax.sharding import PartitionSpec as P

PIECE = 16
LANES = 128
LOW = 16
HIGH = LANES // LOW
ROWS = 2048
COLS = 4096
SCALE = 1.0 / math.sqrt(ROWS * COLS)
GROUP = 16
F32 = jnp.float32
BF16 = jnp.bfloat16
NT = (((1,), (1,)), ((), ()))


def iota(shape, dim):
    return lax.broadcasted_iota(jnp.int32, shape, dim)


def turn(m, modulus):
    quarter = modulus // 4
    quadrant = (m + quarter // 2) // quarter if quarter & (quarter - 1) else (
        lax.shift_right_logical(m + quarter // 2, int(math.log2(quarter))))
    x = (m - quadrant * quarter).astype(F32) * (2.0 * math.pi / modulus)
    y = x * x
    s = x + x * y * (-1.0 / 6 + y * (1.0 / 120 + y * (-1.0 / 5040 + y * (1.0 / 362880))))
    c = 1.0 + y * (-0.5 + y * (1.0 / 24 + y * (-1.0 / 720 + y * (1.0 / 40320))))
    swap = (quadrant & 1) == 1
    cos = jnp.where(swap, s, c)
    sin = jnp.where(swap, c, s)
    cos = jnp.where(((quadrant + 1) & 2) == 2, -cos, cos)
    sin = jnp.where((quadrant & 2) == 2, -sin, sin)
    return cos, sin


def halves(value):
    high = value.astype(BF16)
    return high, (value - high.astype(F32)).astype(BF16)


def column(row):
    return jnp.transpose(jnp.broadcast_to(row, (LANES, LANES)))


def bin_kernel(
    rows_own, col_blocks,
    own_ref, before_ref, after_ref, taps_ref, plate_ref, angle_ref, weight_ref, pixel_ref, owner_ref, block_ref,
    out_ref,
    window, stokes, high_ref, low_ref, left, right,
):
    samples, dets = own_ref.shape
    groups = dets // LANES
    reach = before_ref.shape[0]
    window[:reach] = before_ref[...]
    window[reach : reach + samples] = own_ref[...]
    window[reach + samples :] = after_ref[...]
    width = taps_ref.shape[1]
    band = pltpu.roll(
        jnp.broadcast_to(taps_ref[...], (LANES, width)), 0, axis=1, stride=1, stride_axis=0
    ).astype(BF16)
    twice = 2.0 * angle_ref[...]
    cos_det, sin_det = jnp.cos(twice), jnp.sin(twice)
    quad = 4.0 * plate_ref[...]
    cos_plate, sin_plate = jnp.cos(quad), jnp.sin(quad)
    for part in range(samples // LANES):
        span = slice(part * LANES, (part + 1) * LANES)
        filtered = jnp.dot(
            band, window[part * LANES : part * LANES + width, :], preferred_element_type=F32
        )
        weighted = filtered * weight_ref[...]
        cos_p = jnp.concatenate([column(cos_plate[part : part + 1])] * groups, axis=1)
        sin_p = jnp.concatenate([column(sin_plate[part : part + 1])] * groups, axis=1)
        stokes[0, span] = weighted.astype(BF16).astype(F32)
        stokes[1, span] = (weighted * (cos_p * cos_det - sin_p * sin_det)).astype(BF16).astype(F32)
        stokes[2, span] = (weighted * (sin_p * cos_det + cos_p * sin_det)).astype(BF16).astype(F32)
    pixels = pixel_ref[...]
    high_ref[...] = lax.shift_right_logical(pixels, int(math.log2(LOW)))
    low_ref[...] = pixels & (LOW - 1)
    high_ids = iota((HIGH, dets), 0)
    low_ids = iota((LOW, dets), 0)
    pieces = GROUP // groups

    def group_step(g, carry):
        def piece_step(p, inner):
            first = (g * pieces + p) * PIECE
            for t in range(PIECE):
                row = pl.ds(first + t, 1)
                lanes = slice(t * LANES, (t + 1) * LANES)
                hot = jnp.broadcast_to(high_ref[row, :], (HIGH, dets)) == high_ids
                for s in range(3):
                    spread = jnp.where(hot, jnp.broadcast_to(stokes[s, row, :], (HIGH, dets)), 0.0)
                    both = jnp.concatenate(
                        [spread[:, k * LANES : (k + 1) * LANES] for k in range(groups)], axis=0
                    )
                    at = pl.multiple_of(p * (groups * HIGH), groups * HIGH)
                    left[s, pl.ds(at, groups * HIGH), lanes] = both.astype(BF16)
                low = jnp.where(
                    jnp.broadcast_to(low_ref[row, :], (LOW, dets)) == low_ids, 1.0, 0.0
                ).astype(BF16)
                for k in range(groups):
                    at = pl.multiple_of((p * groups + k) * LOW, LOW)
                    right[pl.ds(at, LOW), lanes] = low[:, k * LANES : (k + 1) * LANES]
            return inner

        lax.fori_loop(0, pieces, piece_step, 0)
        for s in range(3):
            sums = lax.dot_general(left[s], right[...], NT, preferred_element_type=F32)
            mine = lax.div(iota((HIGH, LANES), 1), LOW) == iota((HIGH, LANES), 0)
            rows = []
            for i in range(GROUP):
                start = (i * LOW) // LANES * LANES
                part = sums[i * HIGH : (i + 1) * HIGH, start : start + LANES]
                if start != i * LOW:
                    part = pltpu.roll(part, (start - i * LOW) % LANES, axis=1)
                part = pltpu.roll(part, 0, axis=1, stride=LOW, stride_axis=0)
                rows.append(jnp.sum(jnp.where(mine, part, 0.0), axis=0, keepdims=True))
            out_ref[pl.ds(pl.multiple_of(g * GROUP, GROUP), GROUP), s * LANES : (s + 1) * LANES] = (
                jnp.concatenate(rows, axis=0)
            )
        return carry

    tiles = owner_ref.shape[1]
    lax.fori_loop(0, tiles // GROUP, group_step, 0)
    block = block_ref[...]
    shift = int(math.log2(col_blocks))
    map_row = owner_ref[...] * rows_own + lax.shift_right_logical(block, shift)
    map_col = block & (col_blocks - 1)
    out_ref[tiles:] = jnp.zeros_like(out_ref[tiles:])
    for k, index in ((0, map_row), (1, map_col)):
        twin = jnp.concatenate([index, index], axis=1).astype(F32)
        out_ref[tiles + k : tiles + k + 1, : 2 * tiles] = twin


def spectrum_kernel(
    count, chunks, parts, passes,
    first_ref, mine_ref, other_ref, wiener_ref,
    out_ref,
    tiles, turns, cosine, sine, phase_cos, phase_sin, total,
):
    step = pl.program_id(0) * pl.num_programs(1) + pl.program_id(1)
    chunk = pl.program_id(2)
    kx_block = wiener_ref.shape[1]
    width = parts * LANES
    half = ROWS // 2
    held = LANES // 2
    repeat = phase_cos.shape[0]

    @pl.when(step == 0)
    def _():
        for at in range(0, count, LANES):
            size = min(LANES, count - at)
            kx = first_ref[0] + at + iota((size, LANES), 0)
            c, s = turn((kx * iota((size, LANES), 1)) & (COLS - 1), COLS)
            c, s = c * SCALE, s * SCALE
            high, low = halves(c)
            turns[0, at : at + size, :LANES] = high
            turns[0, at : at + size, LANES:] = low
            high, low = halves(-s)
            turns[1, at : at + size, :LANES] = high
            turns[1, at : at + size, LANES:] = low

    def build():
        left_side = iota((1, LANES), 1) < held
        for p in range(parts):
            rows = slice(p * LANES, (p + 1) * LANES)
            tiles[p * LANES : p * LANES + held] = mine_ref[p, :held]
            tiles[p * LANES + held : (p + 1) * LANES] = other_ref[p, :held]
            r = jnp.where(left_side, mine_ref[p, held : held + 1, :LANES], other_ref[p, held : held + 1, :LANES])
            b = jnp.where(left_side, mine_ref[p, held + 1 : held + 2, :LANES], other_ref[p, held + 1 : held + 2, :LANES])
            ri, bi = r.astype(jnp.int32), b.astype(jnp.int32)
            kx = first_ref[0] + iota((repeat, LANES), 0)
            c, s = turn((ri - kx * bi * LANES) & (2 * ROWS - 1), 2 * ROWS)
            phase_cos[:, rows] = c
            phase_sin[:, rows] = s
            down = column(r).astype(jnp.int32)
            c, s = turn((down * (2 * iota((LANES, LANES), 1) + 1)) & (2 * ROWS - 1), 2 * ROWS)
            cs, ss = turn((down * (2 * LANES)) & (2 * ROWS - 1), 2 * ROWS)
            for at in range(0, half, LANES):
                cosine[rows, at : at + LANES] = c.astype(BF16)
                sine[rows, at : at + LANES] = s.astype(BF16)
                c, s = c * cs - s * ss, c * ss + s * cs

    if chunks == 1:
        pl.when(step == 0)(build)
    else:
        build()

    stokes = pl.program_id(0)
    data = tiles[:, pl.ds(pl.multiple_of(stokes * LANES, LANES), LANES)]
    high, low = halves(data)
    twice = jnp.concatenate([high, high], axis=1)
    at = pl.multiple_of(pl.program_id(1) * kx_block, kx_block)

    def columns(k):
        table = turns[k, pl.ds(at, kx_block), :]
        y = lax.dot_general(table, twice, NT, preferred_element_type=F32)
        return y + lax.dot_general(table[:, :LANES], low, NT, preferred_element_type=F32)

    real, imag = columns(0), columns(1)
    pc = jnp.concatenate([phase_cos[...]] * (kx_block // repeat), axis=0)
    ps = jnp.concatenate([phase_sin[...]] * (kx_block // repeat), axis=0)
    rows = jnp.concatenate([real * pc - imag * ps, real * ps + imag * pc], axis=0)
    split = halves(rows) if passes == 2 else (rows.astype(BF16),)
    chunk_width = 2 * LANES
    flip = LANES - 1 - iota((kx_block, LANES), 1)

    def reverse(value):
        pieces = [
            jnp.take_along_axis(value[:, k : k + LANES], flip, axis=1)
            for k in range(0, value.shape[1], LANES)
        ]
        return jnp.concatenate(pieces[::-1], axis=1)

    for n in range(0, half, chunk_width):
        lanes = slice(n, n + chunk_width)
        back = slice(ROWS - n - chunk_width, ROWS - n)
        even = sum(jnp.dot(part, cosine[:, lanes], preferred_element_type=F32) for part in split)
        odd = sum(jnp.dot(part, sine[:, lanes], preferred_element_type=F32) for part in split)
        re_even, im_even = even[:kx_block], even[kx_block:]
        re_odd, im_odd = odd[:kx_block], odd[kx_block:]
        values = (
            (0, lanes, re_even + im_odd), (1, lanes, im_even - re_odd),
            (0, back, reverse(re_even - im_odd)), (1, back, reverse(im_even + re_odd)),
        )
        for k, where, value in values:
            if chunks == 1:
                out_ref[k, 0, :, where] = value * wiener_ref[0, :, where]
            else:
                @pl.when(chunk == 0)
                def _():
                    total[k, :, where] = value

                @pl.when(chunk > 0)
                def _():
                    total[k, :, where] += value

    if chunks > 1:
        @pl.when(chunk == chunks - 1)
        def _():
            for k in range(2):
                out_ref[k, 0] = total[k] * wiener_ref[0]


def neighbours(value, axis):
    size = lax.axis_size(axis)
    up = [(i, i + 1) for i in range(size - 1)]
    return lax.ppermute(value, axis, up), lax.ppermute(value, axis, [(j, i) for i, j in up])


def gather(value, axis):
    size = lax.axis_size(axis)
    if size // 2 > 8:
        whole = lax.all_gather(value, axis, axis=0)
        return whole[: size // 2], whole[size // 2 :]
    found = [value] + [
        lax.ppermute(value, axis, [(i, (i + 2 * k) % size) for i in range(size)])
        for k in range(1, size // 2)
    ]
    mine = jnp.stack(found)
    return mine, lax.ppermute(mine, axis, [(i, i ^ 1) for i in range(size)])


def body(
    timeline, pointing, plate_angle, detector_angle, detector_weight, kernel, tile_owner, tile_block, wiener
):
    samples, dets = timeline.shape
    tiles = tile_owner.shape[0]
    devices = lax.axis_size("tm")
    before, after = neighbours(timeline, "tm")
    count_taps = kernel.shape[0]
    reach = (count_taps - 1) // 2
    before, after = before[samples - reach :], after[:reach]
    width = count_taps - 1 + LANES
    taps = jnp.pad(kernel.astype(F32), (0, width - count_taps)).reshape(1, width)
    plate = jnp.pad(plate_angle.reshape(samples // LANES, LANES), ((0, 8 - samples // LANES), (0, 0)))
    rows_own = ROWS // devices
    col_blocks = COLS // LANES
    packed = pl.pallas_call(
        functools.partial(bin_kernel, rows_own, col_blocks),
        out_shape=jax.ShapeDtypeStruct((tiles + 8, 3 * LANES), F32),
        scratch_shapes=[
            pltpu.VMEM((2 * reach + samples, dets), BF16),
            pltpu.VMEM((3, samples, dets), F32),
            pltpu.VMEM((samples, dets), jnp.int32),
            pltpu.VMEM((samples, dets), jnp.int32),
            pltpu.VMEM((3, GROUP * HIGH, PIECE * LANES), BF16),
            pltpu.VMEM((GROUP * LOW, PIECE * LANES), BF16),
        ],
        name="bin_tiles",
    )(
        timeline, before, after, taps, plate, detector_angle.reshape(1, dets), detector_weight.reshape(1, dets),
        pointing, tile_owner.reshape(1, tiles), tile_block.reshape(1, tiles),
    )
    mine, other = gather(packed, "tm")
    stokes, count, ky = wiener.shape
    total_parts = mine.shape[0]
    parts = min(4, total_parts)
    chunks = total_parts // parts
    kx_block = min(128, count)
    repeat = min(COLS // LANES, kx_block)
    passes = 2
    first = (lax.axis_index("tm") * count).astype(jnp.int32).reshape(1)
    piece = pl.BlockSpec((parts, tiles + 8, 3 * LANES), lambda s, k, c, _: (c, 0, 0))
    return pl.pallas_call(
        functools.partial(spectrum_kernel, count, chunks, parts, passes),
        grid_spec=pltpu.PrefetchScalarGridSpec(
            num_scalar_prefetch=1,
            grid=(stokes, count // kx_block, chunks),
            in_specs=[piece, piece, pl.BlockSpec((1, kx_block, ky), lambda s, k, c, _: (s, k, 0))],
            out_specs=pl.BlockSpec((2, 1, kx_block, ky), lambda s, k, c, _: (0, s, k, 0)),
            scratch_shapes=[
                pltpu.VMEM((parts * LANES, 3 * LANES), F32),
                pltpu.VMEM((2, count, 2 * LANES), BF16),
                pltpu.VMEM((parts * LANES, ROWS // 2), BF16),
                pltpu.VMEM((parts * LANES, ROWS // 2), BF16),
                pltpu.VMEM((repeat, parts * LANES), F32),
                pltpu.VMEM((repeat, parts * LANES), F32),
                pltpu.VMEM((2, kx_block, ky) if chunks > 1 else (8, LANES), F32),
            ],
        ),
        out_shape=jax.ShapeDtypeStruct((2, stokes, count, ky), F32),
        name="spectra",
    )(first, mine, other, wiener)


def solution(mesh):
    placed = (
        P("tm", "band"), P("tm", "band"), P("tm"), P("band"), P("band"), P("band"),
        P("tm", "band"), P("tm", "band"), P("band", "tm", None),
    )
    return jax.shard_map(
        body, mesh=mesh, in_specs=placed, out_specs=P(None, "band", "tm", None), check_vma=False
    )
```

```python
import functools
import math

import jax
import jax.numpy as jnp
from jax import lax
from jax.experimental import pallas as pl
from jax.experimental.pallas import tpu as pltpu
from jax.sharding import PartitionSpec as P

PIECE = 16
LANES = 128
LOW = 16
HIGH = LANES // LOW
ROWS = 2048
COLS = 4096
SCALE = 1.0 / math.sqrt(ROWS * COLS)
GROUP = 16
F32 = jnp.float32
BF16 = jnp.bfloat16
NT = (((1,), (1,)), ((), ()))


def iota(shape, dim):
    return lax.broadcasted_iota(jnp.int32, shape, dim)


def turn(m, modulus):
    quarter = modulus // 4
    quadrant = (m + quarter // 2) // quarter if quarter & (quarter - 1) else (
        lax.shift_right_logical(m + quarter // 2, int(math.log2(quarter))))
    x = (m - quadrant * quarter).astype(F32) * (2.0 * math.pi / modulus)
    y = x * x
    s = x + x * y * (-1.0 / 6 + y * (1.0 / 120 + y * (-1.0 / 5040 + y * (1.0 / 362880))))
    c = 1.0 + y * (-0.5 + y * (1.0 / 24 + y * (-1.0 / 720 + y * (1.0 / 40320))))
    swap = (quadrant & 1) == 1
    cos = jnp.where(swap, s, c)
    sin = jnp.where(swap, c, s)
    cos = jnp.where(((quadrant + 1) & 2) == 2, -cos, cos)
    sin = jnp.where((quadrant & 2) == 2, -sin, sin)
    return cos, sin


def halves(value):
    high = value.astype(BF16)
    return high, (value - high.astype(F32)).astype(BF16)


def column(row):
    return jnp.transpose(jnp.broadcast_to(row, (LANES, LANES)))


def bin_kernel(
    rows_own, col_blocks,
    own_ref, before_ref, after_ref, taps_ref, plate_ref, angle_ref, weight_ref, pixel_ref, owner_ref, block_ref,
    out_ref,
    window, stokes, high_ref, low_ref, left, right,
):
    samples, dets = own_ref.shape
    groups = dets // LANES
    reach = before_ref.shape[0]
    window[:reach] = before_ref[...]
    window[reach : reach + samples] = own_ref[...]
    window[reach + samples :] = after_ref[...]
    width = taps_ref.shape[1]
    band = pltpu.roll(
        jnp.broadcast_to(taps_ref[...], (LANES, width)), 0, axis=1, stride=1, stride_axis=0
    ).astype(BF16)
    twice = 2.0 * angle_ref[...]
    cos_det, sin_det = jnp.cos(twice), jnp.sin(twice)
    quad = 4.0 * plate_ref[...]
    cos_plate, sin_plate = jnp.cos(quad), jnp.sin(quad)
    for part in range(samples // LANES):
        span = slice(part * LANES, (part + 1) * LANES)
        filtered = jnp.dot(
            band, window[part * LANES : part * LANES + width, :], preferred_element_type=F32
        )
        weighted = filtered * weight_ref[...]
        cos_p = jnp.concatenate([column(cos_plate[part : part + 1])] * groups, axis=1)
        sin_p = jnp.concatenate([column(sin_plate[part : part + 1])] * groups, axis=1)
        stokes[0, span] = weighted.astype(BF16).astype(F32)
        stokes[1, span] = (weighted * (cos_p * cos_det - sin_p * sin_det)).astype(BF16).astype(F32)
        stokes[2, span] = (weighted * (sin_p * cos_det + cos_p * sin_det)).astype(BF16).astype(F32)
    pixels = pixel_ref[...]
    high_ref[...] = lax.shift_right_logical(pixels, int(math.log2(LOW)))
    low_ref[...] = pixels & (LOW - 1)
    high_ids = iota((HIGH, dets), 0)
    low_ids = iota((LOW, dets), 0)
    pieces = GROUP // groups

    def group_step(g, carry):
        def piece_step(p, inner):
            first = (g * pieces + p) * PIECE
            for t in range(PIECE):
                row = pl.ds(first + t, 1)
                lanes = slice(t * LANES, (t + 1) * LANES)
                hot = jnp.broadcast_to(high_ref[row, :], (HIGH, dets)) == high_ids
                for s in range(3):
                    spread = jnp.where(hot, jnp.broadcast_to(stokes[s, row, :], (HIGH, dets)), 0.0)
                    both = jnp.concatenate(
                        [spread[:, k * LANES : (k + 1) * LANES] for k in range(groups)], axis=0
                    )
                    at = pl.multiple_of(p * (groups * HIGH), groups * HIGH)
                    left[s, pl.ds(at, groups * HIGH), lanes] = both.astype(BF16)
                low = jnp.where(
                    jnp.broadcast_to(low_ref[row, :], (LOW, dets)) == low_ids, 1.0, 0.0
                ).astype(BF16)
                for k in range(groups):
                    at = pl.multiple_of((p * groups + k) * LOW, LOW)
                    right[pl.ds(at, LOW), lanes] = low[:, k * LANES : (k + 1) * LANES]
            return inner

        lax.fori_loop(0, pieces, piece_step, 0)
        for s in range(3):
            sums = lax.dot_general(left[s], right[...], NT, preferred_element_type=F32)
            mine = lax.div(iota((HIGH, LANES), 1), LOW) == iota((HIGH, LANES), 0)
            rows = []
            for i in range(GROUP):
                start = (i * LOW) // LANES * LANES
                part = sums[i * HIGH : (i + 1) * HIGH, start : start + LANES]
                if start != i * LOW:
                    part = pltpu.roll(part, (start - i * LOW) % LANES, axis=1)
                part = pltpu.roll(part, 0, axis=1, stride=LOW, stride_axis=0)
                rows.append(jnp.sum(jnp.where(mine, part, 0.0), axis=0, keepdims=True))
            out_ref[pl.ds(pl.multiple_of(g * GROUP, GROUP), GROUP), s * LANES : (s + 1) * LANES] = (
                jnp.concatenate(rows, axis=0)
            )
        return carry

    tiles = owner_ref.shape[1]
    lax.fori_loop(0, tiles // GROUP, group_step, 0)
    block = block_ref[...]
    shift = int(math.log2(col_blocks))
    map_row = owner_ref[...] * rows_own + lax.shift_right_logical(block, shift)
    map_col = block & (col_blocks - 1)
    out_ref[tiles:] = jnp.zeros_like(out_ref[tiles:])
    for k, index in ((0, map_row), (1, map_col)):
        twin = jnp.concatenate([index, index], axis=1).astype(F32)
        out_ref[tiles + k : tiles + k + 1, : 2 * tiles] = twin


def table_kernel(first_ref, wiener_ref, ready_ref, held_ref, turns_ref, sem):
    del ready_ref
    copy = pltpu.make_async_copy(wiener_ref, held_ref, sem)
    copy.start()
    count = turns_ref.shape[1]
    for at in range(0, count, LANES):
        size = min(LANES, count - at)
        kx = first_ref[0] + at + iota((size, LANES), 0)
        c, s = turn((kx * iota((size, LANES), 1)) & (COLS - 1), COLS)
        for k, value in enumerate((c * SCALE, s * -SCALE)):
            high, low = halves(value)
            turns_ref[k, at : at + size, :LANES] = high
            turns_ref[k, at : at + size, LANES:] = low
    copy.wait()


def spectrum_kernel(
    first_ref, mine_ref, other_ref, wiener_ref, turns_ref,
    out_ref,
    tiles, factor, table, base, advance, phases, buffer, sems,
):
    parts = mine_ref.shape[0]
    stokes, count, ky = wiener_ref.shape
    held = LANES // 2
    repeat = phases.shape[1]
    block = min(256, count)
    left_side = iota((1, LANES), 1) < held
    half_turns = 2 * ROWS - 1

    def build(p, carry):
        rows = pl.ds(pl.multiple_of(p * LANES, LANES), LANES)
        low, high = mine_ref.at[p], other_ref.at[p]
        tiles[pl.ds(pl.multiple_of(p * LANES, LANES), held)] = low[:held]
        tiles[pl.ds(pl.multiple_of(p * LANES + held, held), held)] = high[:held]
        r = jnp.where(left_side, low[held : held + 1, :LANES], high[held : held + 1, :LANES])
        b = jnp.where(left_side, low[held + 1 : held + 2, :LANES], high[held + 1 : held + 2, :LANES])
        kx = first_ref[0] + iota((repeat, LANES), 0)
        c, s = turn((r.astype(jnp.int32) - kx * b.astype(jnp.int32) * LANES) & half_turns, 2 * ROWS)
        phases[0, :, rows] = c
        phases[1, :, rows] = s
        down = column(r).astype(jnp.int32)
        c, s = turn((down * (2 * iota((LANES, LANES), 1) + 1)) & half_turns, 2 * ROWS)
        base[0, rows] = c
        base[1, rows] = s
        c, s = turn((down * (2 * LANES)) & half_turns, 2 * ROWS)
        advance[0, rows] = c
        advance[1, rows] = s
        return carry

    lax.fori_loop(0, parts, build, 0, unroll=parts <= 4)
    half = ky // 2

    def spread(n, carry):
        at = pl.ds(pl.multiple_of(n * 2 * LANES, 2 * LANES), LANES)
        under = pl.ds(pl.multiple_of(n * 2 * LANES + LANES, LANES), LANES)
        c, s = base[0], base[1]
        table[:, at] = c.astype(BF16)
        table[:, under] = s.astype(BF16)
        base[0] = c * advance[0] - s * advance[1]
        base[1] = c * advance[1] + s * advance[0]
        return carry

    lax.fori_loop(0, half // LANES, spread, 0)
    width = min(4, parts) * LANES
    flip = LANES - 1 - iota((block, LANES), 1)

    def copies(i, slot):
        s, k = lax.div(i, count // block), lax.rem(i, count // block)
        at = pl.ds(pl.multiple_of(k * block, block), block)
        for side in range(2):
            yield pltpu.make_async_copy(
                buffer.at[slot, side], out_ref.at[side, s, at], sems.at[slot, side]
            )

    def step(i, carry):
        slot = lax.rem(i, 2)
        s, k = lax.div(i, count // block), lax.rem(i, count // block)
        at = pl.ds(pl.multiple_of(k * block, block), block)
        channel = pl.ds(pl.multiple_of(s * LANES, LANES), LANES)

        def make(q, inner):
            rows = pl.ds(pl.multiple_of(q * width, width), width)
            high, low = halves(tiles[rows, channel])
            twice = jnp.concatenate([high, high], axis=1)
            real, imag = [
                lax.dot_general(turns_ref[side, at], twice, NT, preferred_element_type=F32)
                + lax.dot_general(turns_ref[side, at, :LANES], low, NT, preferred_element_type=F32)
                for side in range(2)
            ]
            pc = jnp.concatenate([phases[0, :, rows]] * (block // repeat), axis=0)
            ps = jnp.concatenate([phases[1, :, rows]] * (block // repeat), axis=0)
            factor[:block, rows] = (real * pc - imag * ps).astype(BF16)
            factor[block:, rows] = (real * ps + imag * pc).astype(BF16)
            return inner

        lax.fori_loop(0, parts * LANES // width, make, 0)

        @pl.when(i >= 2)
        def _():
            for copy in copies(i, slot):
                copy.wait()

        for n in range(half // LANES):
            lanes = slice(n * LANES, (n + 1) * LANES)
            back = slice(ky - (n + 1) * LANES, ky - n * LANES)
            both = jnp.dot(
                factor[...], table[:, 2 * n * LANES : 2 * (n + 1) * LANES], preferred_element_type=F32
            )
            re_even, re_odd = both[:block, :LANES], both[:block, LANES:]
            im_even, im_odd = both[block:, :LANES], both[block:, LANES:]
            weight = wiener_ref[s, at, lanes]
            buffer[slot, 0, :, lanes] = (re_even + im_odd) * weight
            buffer[slot, 1, :, lanes] = (im_even - re_odd) * weight
            weight = wiener_ref[s, at, back]
            buffer[slot, 0, :, back] = jnp.take_along_axis(re_even - im_odd, flip, axis=1) * weight
            buffer[slot, 1, :, back] = jnp.take_along_axis(im_even + re_odd, flip, axis=1) * weight
        for copy in copies(i, slot):
            copy.start()
        return carry

    steps = stokes * (count // block)
    lax.fori_loop(0, steps, step, 0)
    for i in (steps - 2, steps - 1):
        for copy in copies(i, i % 2):
            copy.wait()


def neighbours(value, axis):
    size = lax.axis_size(axis)
    up = [(i, i + 1) for i in range(size - 1)]
    return lax.ppermute(value, axis, up), lax.ppermute(value, axis, [(j, i) for i, j in up])


def gather(value, ready, axis):
    size = lax.axis_size(axis)
    if size // 2 > 8:
        whole = lax.all_gather(value, axis, axis=0)
        return whole[: size // 2], whole[size // 2 :]
    found = [
        lax.ppermute(value, axis, [(i, (i + 2 * k) % size) for i in range(size)])
        for k in range(1, size // 2)
    ]
    own, _ = lax.optimization_barrier((value, ready))
    mine = jnp.stack([own] + found)
    return mine, lax.ppermute(mine, axis, [(i, i ^ 1) for i in range(size)])


def body(
    timeline, pointing, plate_angle, detector_angle, detector_weight, kernel, tile_owner, tile_block, wiener
):
    samples, dets = timeline.shape
    tiles = tile_owner.shape[0]
    devices = lax.axis_size("tm")
    before, after = neighbours(timeline, "tm")
    count_taps = kernel.shape[0]
    reach = (count_taps - 1) // 2
    before, after = before[samples - reach :], after[:reach]
    width = count_taps - 1 + LANES
    taps = jnp.pad(kernel.astype(F32), (0, width - count_taps)).reshape(1, width)
    plate = jnp.pad(plate_angle.reshape(samples // LANES, LANES), ((0, 8 - samples // LANES), (0, 0)))
    rows_own = ROWS // devices
    col_blocks = COLS // LANES
    packed = pl.pallas_call(
        functools.partial(bin_kernel, rows_own, col_blocks),
        out_shape=jax.ShapeDtypeStruct((tiles + 8, 3 * LANES), F32),
        scratch_shapes=[
            pltpu.VMEM((2 * reach + samples, dets), BF16),
            pltpu.VMEM((3, samples, dets), F32),
            pltpu.VMEM((samples, dets), jnp.int32),
            pltpu.VMEM((samples, dets), jnp.int32),
            pltpu.VMEM((3, GROUP * HIGH, PIECE * LANES), BF16),
            pltpu.VMEM((GROUP * LOW, PIECE * LANES), BF16),
        ],
        name="bin_tiles",
    )(
        timeline, before, after, taps, plate, detector_angle.reshape(1, dets), detector_weight.reshape(1, dets),
        pointing, tile_owner.reshape(1, tiles), tile_block.reshape(1, tiles),
    )
    stokes, count, ky = wiener.shape
    first = (lax.axis_index("tm") * count).astype(jnp.int32).reshape(1)
    vmem, hbm = pl.BlockSpec(memory_space=pltpu.VMEM), pl.BlockSpec(memory_space=pltpu.HBM)
    scalar = pl.BlockSpec(memory_space=pltpu.SMEM)
    held, turns = pl.pallas_call(
        table_kernel,
        in_specs=[scalar, hbm, pl.BlockSpec(memory_space=pl.ANY)],
        out_specs=[vmem, vmem],
        out_shape=[pltpu.VMEM(wiener.shape, F32), pltpu.VMEM((2, count, 2 * LANES), BF16)],
        scratch_shapes=[pltpu.SemaphoreType.DMA],
        compiler_params=pltpu.CompilerParams(vmem_limit_bytes=4 * 2**20),
        cost_estimate=pl.CostEstimate(flops=0, bytes_accessed=2 * wiener.size * 4, transcendentals=0),
        name="tables",
    )(first, wiener, packed)
    mine, other = gather(packed, turns, "tm")
    parts = min(16, mine.shape[0])
    block = min(256, count)
    repeat = min(COLS // LANES, block)
    every = parts * LANES
    spectra = pl.pallas_call(
        spectrum_kernel,
        in_specs=[scalar, vmem, vmem, vmem, vmem],
        out_specs=hbm,
        scratch_shapes=[
            pltpu.VMEM((every, 3 * LANES), F32),
            pltpu.VMEM((2 * block, every), BF16),
            pltpu.VMEM((every, ky), BF16),
            pltpu.VMEM((2, every, LANES), F32),
            pltpu.VMEM((2, every, LANES), F32),
            pltpu.VMEM((2, repeat, every), F32),
            pltpu.VMEM((2, 2, block, ky), F32),
            pltpu.SemaphoreType.DMA((2, 2)),
        ],
        out_shape=jax.ShapeDtypeStruct((2, stokes, count, ky), F32),
        compiler_params=pltpu.CompilerParams(vmem_limit_bytes=40 * 2**20),
        name="spectra",
    )
    held = pltpu.with_memory_space_constraint(held, pltpu.VMEM)
    turns = pltpu.with_memory_space_constraint(turns, pltpu.VMEM)
    return sum(
        spectra(first, mine[at : at + parts], other[at : at + parts], held, turns)
        for at in range(0, mine.shape[0], parts)
    )


def solution(mesh):
    placed = (
        P("tm", "band"), P("tm", "band"), P("tm"), P("band"), P("band"), P("band"),
        P("tm", "band"), P("tm", "band"), P("band", "tm", None),
    )
    return jax.shard_map(
        body, mesh=mesh, in_specs=placed, out_specs=P(None, "band", "tm", None), check_vma=False
    )
```

```python
import functools
import math

import jax
import jax.numpy as jnp
from jax import lax
from jax.experimental import pallas as pl
from jax.experimental.pallas import tpu as pltpu
from jax.sharding import PartitionSpec as P

PIECE = 16
LANES = 128
LOW = 16
HIGH = LANES // LOW
ROWS = 2048
COLS = 4096
SCALE = 1.0 / math.sqrt(ROWS * COLS)
GROUP = 16
F32 = jnp.float32
BF16 = jnp.bfloat16
NT = (((1,), (1,)), ((), ()))


def iota(shape, dim):
    return lax.broadcasted_iota(jnp.int32, shape, dim)


def turn(m, modulus):
    quarter = modulus // 4
    quadrant = (m + quarter // 2) // quarter if quarter & (quarter - 1) else (
        lax.shift_right_logical(m + quarter // 2, int(math.log2(quarter))))
    x = (m - quadrant * quarter).astype(F32) * (2.0 * math.pi / modulus)
    y = x * x
    s = x + x * y * (-1.0 / 6 + y * (1.0 / 120 + y * (-1.0 / 5040 + y * (1.0 / 362880))))
    c = 1.0 + y * (-0.5 + y * (1.0 / 24 + y * (-1.0 / 720 + y * (1.0 / 40320))))
    swap = (quadrant & 1) == 1
    cos = jnp.where(swap, s, c)
    sin = jnp.where(swap, c, s)
    cos = jnp.where(((quadrant + 1) & 2) == 2, -cos, cos)
    sin = jnp.where((quadrant & 2) == 2, -sin, sin)
    return cos, sin


def halves(value):
    high = value.astype(BF16)
    return high, (value - high.astype(F32)).astype(BF16)


def column(row):
    return jnp.transpose(jnp.broadcast_to(row, (LANES, LANES)))


def prepare_kernel(
    rows_own, col_blocks, tiles,
    pixel_ref, time_ref, small_ref,
    band_ref, factor_ref, high_ref, right_ref, own_ref, index_ref,
    low_ref,
):
    samples, dets = pixel_ref.shape
    groups = dets // LANES
    pieces = GROUP // groups
    width = band_ref.shape[1]
    own_ref[...] = time_ref[...]
    lines = [width // LANES, samples // LANES, groups, groups]
    starts = [sum(lines[:k]) for k in range(5)]

    def row(k):
        return jnp.concatenate(
            [small_ref[i : i + 1] for i in range(starts[k], starts[k] + lines[k])], axis=1
        )

    band_ref[...] = pltpu.roll(
        jnp.broadcast_to(row(0), (LANES, width)), 0, axis=1, stride=1, stride_axis=0
    ).astype(BF16)
    angle, weight = row(2), row(3)
    cos_det, sin_det = jnp.cos(2.0 * angle) * weight, jnp.sin(2.0 * angle) * weight
    quad = 4.0 * small_ref[starts[1] : starts[1] + lines[1]]
    cos_plate, sin_plate = jnp.cos(quad), jnp.sin(quad)
    for part in range(samples // LANES):
        span = slice(part * LANES, (part + 1) * LANES)
        cos_p = jnp.concatenate([column(cos_plate[part : part + 1])] * groups, axis=1)
        sin_p = jnp.concatenate([column(sin_plate[part : part + 1])] * groups, axis=1)
        factor_ref[0, span] = jnp.broadcast_to(weight, (LANES, dets))
        factor_ref[1, span] = cos_p * cos_det - sin_p * sin_det
        factor_ref[2, span] = sin_p * cos_det + cos_p * sin_det
    last = small_ref[starts[4] : starts[4] + 1]
    owner, block = last[:, :tiles].astype(jnp.int32), last[:, tiles : 2 * tiles].astype(jnp.int32)
    shift = int(math.log2(col_blocks))
    map_row = owner * rows_own + lax.shift_right_logical(block, shift)
    map_col = block & (col_blocks - 1)
    index_ref[...] = jnp.zeros_like(index_ref)
    for k, index in ((0, map_row), (1, map_col)):
        index_ref[k : k + 1, : 2 * tiles] = jnp.concatenate([index, index], axis=1).astype(F32)
    pixels = pixel_ref[...]
    high_ref[...] = lax.shift_right_logical(pixels, int(math.log2(LOW)))
    low_ref[...] = pixels & (LOW - 1)
    low_ids = iota((LOW, dets), 0)

    def piece_step(q, carry):
        g, p = lax.div(q, pieces), lax.rem(q, pieces)
        for t in range(PIECE):
            lanes = slice(t * LANES, (t + 1) * LANES)
            row = pl.ds(q * PIECE + t, 1)
            low = jnp.where(
                jnp.broadcast_to(low_ref[row, :], (LOW, dets)) == low_ids, 1.0, 0.0
            ).astype(BF16)
            for k in range(groups):
                at = pl.multiple_of((p * groups + k) * LOW, LOW)
                right_ref[g, pl.ds(at, LOW), lanes] = low[:, k * LANES : (k + 1) * LANES]
        return carry

    lax.fori_loop(0, samples // PIECE, piece_step, 0)


def bin_kernel(
    reach,
    place_ref, partner_ref, outside_ref, band_ref, factor_ref, high_ref, right_ref, own_ref, index_ref,
    out_ref,
    window, stokes, left,
):
    samples, dets = own_ref.shape
    groups = dets // LANES
    is_first = lax.rem(place_ref[0], 2) == 0
    window[reach : reach + samples] = own_ref[...]

    @pl.when(is_first)
    def _():
        window[:reach] = outside_ref[samples - reach :]
        window[reach + samples :] = partner_ref[:reach]

    @pl.when(jnp.logical_not(is_first))
    def _():
        window[:reach] = partner_ref[samples - reach :]
        window[reach + samples :] = outside_ref[:reach]

    width = band_ref.shape[1]
    for part in range(samples // LANES):
        span = slice(part * LANES, (part + 1) * LANES)
        filtered = jnp.dot(
            band_ref[...], window[part * LANES : part * LANES + width, :], preferred_element_type=F32
        )
        for s in range(3):
            stokes[s, span] = (filtered * factor_ref[s, span]).astype(BF16).astype(F32)
    high_ids = iota((HIGH, dets), 0)
    pieces = GROUP // groups
    mine = lax.div(iota((HIGH, LANES), 1), LOW) == iota((HIGH, LANES), 0)
    stack = GROUP * HIGH

    def group_step(g, carry):
        def piece_step(p, inner):
            first = (g * pieces + p) * PIECE
            for t in range(PIECE):
                row = pl.ds(first + t, 1)
                lanes = slice(t * LANES, (t + 1) * LANES)
                hot = jnp.broadcast_to(high_ref[row, :], (HIGH, dets)) == high_ids
                for s in range(3):
                    spread = jnp.where(hot, jnp.broadcast_to(stokes[s, row, :], (HIGH, dets)), 0.0)
                    both = jnp.concatenate(
                        [spread[:, k * LANES : (k + 1) * LANES] for k in range(groups)], axis=0
                    )
                    at = pl.multiple_of(s * stack + p * (groups * HIGH), groups * HIGH)
                    left[pl.ds(at, groups * HIGH), lanes] = both.astype(BF16)
            return inner

        lax.fori_loop(0, pieces, piece_step, 0)
        sums = lax.dot_general(left[...], right_ref[g], NT, preferred_element_type=F32)
        for s in range(3):
            rows = []
            for i in range(GROUP):
                start = (i * LOW) // LANES * LANES
                part = sums[s * stack + i * HIGH : s * stack + (i + 1) * HIGH, start : start + LANES]
                if start != i * LOW:
                    part = pltpu.roll(part, (start - i * LOW) % LANES, axis=1)
                part = pltpu.roll(part, 0, axis=1, stride=LOW, stride_axis=0)
                rows.append(jnp.sum(jnp.where(mine, part, 0.0), axis=0, keepdims=True))
            out_ref[pl.ds(pl.multiple_of(g * GROUP, GROUP), GROUP), s * LANES : (s + 1) * LANES] = (
                jnp.concatenate(rows, axis=0)
            )
        return carry

    tiles = out_ref.shape[0] - index_ref.shape[0]
    lax.fori_loop(0, tiles // GROUP, group_step, 0)
    out_ref[tiles:] = index_ref[...]


def table_kernel(place_ref, wiener_ref, ready_ref, held_ref, turns_ref, sem):
    del ready_ref
    copy = pltpu.make_async_copy(wiener_ref, held_ref, sem)
    copy.start()
    count = turns_ref.shape[1]
    first = place_ref[0] * count
    for at in range(0, count, LANES):
        size = min(LANES, count - at)
        kx = first + at + iota((size, LANES), 0)
        c, s = turn((kx * iota((size, LANES), 1)) & (COLS - 1), COLS)
        for k, value in enumerate((c * SCALE, s * -SCALE)):
            high, low = halves(value)
            turns_ref[k, at : at + size, :LANES] = high
            turns_ref[k, at : at + size, LANES:] = low
    copy.wait()


def expand(first, stack_ref, tiles, phases, table, start):
    parts = stack_ref.shape[0] // 2
    held = LANES // 2
    repeat = phases.shape[1]
    ky = table.shape[1]
    left_side = iota((1, LANES), 1) < held
    half_turns = 2 * ROWS - 1

    def build(p, carry):
        rows = pl.ds(pl.multiple_of(p * LANES, LANES), LANES)
        low, high = stack_ref.at[2 * p], stack_ref.at[2 * p + 1]
        tiles[pl.ds(pl.multiple_of(p * LANES, LANES), held)] = low[:held]
        tiles[pl.ds(pl.multiple_of(p * LANES + held, held), held)] = high[:held]
        r = jnp.where(left_side, low[held : held + 1, :LANES], high[held : held + 1, :LANES])
        b = jnp.where(left_side, low[held + 1 : held + 2, :LANES], high[held + 1 : held + 2, :LANES])
        kx = first + iota((repeat, LANES), 0)
        c, s = turn((r.astype(jnp.int32) - kx * b.astype(jnp.int32) * LANES) & half_turns, 2 * ROWS)
        phases[0, :, rows] = c
        phases[1, :, rows] = s
        down = column(r).astype(jnp.int32)
        c, s = turn((r.astype(jnp.int32) * (2 * LANES)) & half_turns, 2 * ROWS)
        turn_c, turn_s = column(c), column(s)
        for g in range(0, LANES, 16):
            some = slice(g, g + 16)
            c, s = turn((down[some] * (2 * iota((16, LANES), 1) + 1)) & half_turns, 2 * ROWS)
            cs, ss = turn_c[some], turn_s[some]
            at = pl.ds(pl.multiple_of(start + p * LANES + g, 16), 16)
            for n in range(0, ky, 2 * LANES):
                table[at, n : n + LANES] = c.astype(BF16)
                table[at, n + LANES : n + 2 * LANES] = s.astype(BF16)
                c, s = c * cs - s * ss, c * ss + s * cs
        return carry

    lax.fori_loop(0, parts, build, 0, unroll=parts <= 4)


def factors(tiles, phases, turns_ref, rows, channel, at, size):
    high, low = halves(tiles[rows, channel])
    twice = jnp.concatenate([high, high], axis=1)
    real, imag = [
        lax.dot_general(turns_ref[side, at], twice, NT, preferred_element_type=F32)
        + lax.dot_general(turns_ref[side, at, :LANES], low, NT, preferred_element_type=F32)
        for side in range(2)
    ]
    pc = jnp.concatenate([phases[0, :, rows]] * (size // phases.shape[1]), axis=0)
    ps = jnp.concatenate([phases[1, :, rows]] * (size // phases.shape[1]), axis=0)
    return (real * pc - imag * ps).astype(BF16), (real * ps + imag * pc).astype(BF16)


def early_kernel(block, place_ref, stack_ref, turns_ref, factor_ref, table_ref, tiles, phases):
    stokes, count = factor_ref.shape[0], factor_ref.shape[1] // 2
    expand(place_ref[0] * count, stack_ref, tiles, phases, table_ref, 0)
    for s in range(stokes):
        channel = slice(s * LANES, (s + 1) * LANES)
        for k in range(0, count, block):
            real, imag = factors(
                tiles, phases, turns_ref, slice(None), channel, slice(k, k + block), block
            )
            factor_ref[s, k : k + block] = real
            factor_ref[s, count + k : count + k + block] = imag


def spectrum_kernel(early, place_ref, stack_ref, wiener_ref, turns_ref, *refs):
    ready_factor, ready_table = refs[:2] if early else (None, None)
    out_ref, tiles, factor, table, phases, buffer, sems = refs[2 * early :]
    stokes, count, ky = wiener_ref.shape
    block = factor.shape[0] // 2
    own = tiles.shape[0]
    ready = table.shape[0] - own
    if early:
        table[:ready] = ready_table[...]
    expand(place_ref[0] * count, stack_ref, tiles, phases, table, ready)
    half = ky // 2
    width = min(4 * LANES, own)
    flip = LANES - 1 - iota((block, LANES), 1)

    quarter = half // 2
    spans = ((0, quarter), (ky - quarter, quarter), (quarter, half))

    def copies(i, slot, which):
        s, k = lax.div(i, count // block), lax.rem(i, count // block)
        at = pl.ds(pl.multiple_of(k * block, block), block)
        for j in which:
            lanes = pl.ds(*spans[j])
            for side in range(2):
                yield pltpu.make_async_copy(
                    buffer.at[slot, side, :, lanes], out_ref.at[side, s, at, lanes], sems.at[slot, side, j]
                )

    def step(i, carry):
        slot = lax.rem(i, 2)
        s, k = lax.div(i, count // block), lax.rem(i, count // block)
        at = pl.ds(pl.multiple_of(k * block, block), block)
        channel = pl.ds(pl.multiple_of(s * LANES, LANES), LANES)

        def make(q, inner):
            rows = pl.ds(pl.multiple_of(q * width, width), width)
            into = pl.ds(pl.multiple_of(ready + q * width, LANES), width)
            real, imag = factors(tiles, phases, turns_ref, rows, channel, at, block)
            factor[:block, into] = real
            factor[block:, into] = imag
            return inner

        lax.fori_loop(0, own // width, make, 0)
        if early:
            under = pl.ds(pl.multiple_of(count + k * block, block), block)
            factor[:block, :ready] = ready_factor[s, at]
            factor[block:, :ready] = ready_factor[s, under]

        @pl.when(i >= 2)
        def _():
            for copy in copies(i, slot, (0, 1, 2)):
                copy.wait()

        for n in range(half // LANES):
            lanes = slice(n * LANES, (n + 1) * LANES)
            back = slice(ky - (n + 1) * LANES, ky - n * LANES)
            both = jnp.dot(
                factor[...], table[:, 2 * n * LANES : 2 * (n + 1) * LANES], preferred_element_type=F32
            )
            re_even, re_odd = both[:block, :LANES], both[:block, LANES:]
            im_even, im_odd = both[block:, :LANES], both[block:, LANES:]
            weight = wiener_ref[s, at, lanes]
            buffer[slot, 0, :, lanes] = (re_even + im_odd) * weight
            buffer[slot, 1, :, lanes] = (im_even - re_odd) * weight
            weight = wiener_ref[s, at, back]
            buffer[slot, 0, :, back] = jnp.take_along_axis(re_even - im_odd, flip, axis=1) * weight
            buffer[slot, 1, :, back] = jnp.take_along_axis(im_even + re_odd, flip, axis=1) * weight
            if (n + 1) * LANES == quarter:
                for copy in copies(i, slot, (0, 1)):
                    copy.start()
        for copy in copies(i, slot, (2,)):
            copy.start()
        return carry

    steps = stokes * (count // block)
    lax.fori_loop(0, steps, step, 0)
    for i in (steps - 2, steps - 1):
        for copy in copies(i, i % 2, (0, 1, 2)):
            copy.wait()


def neighbours(value, axis):
    size = lax.axis_size(axis)
    outer = [(i, i + 1) for i in range(1, size - 1, 2)]
    outside = lax.ppermute(value, axis, outer + [(j, i) for i, j in outer])
    return lax.ppermute(value, axis, [(i, i ^ 1) for i in range(size)]), outside


def gather(value, ready, axis):
    size = lax.axis_size(axis)
    most = 32
    if size > 8:
        whole = lax.all_gather(value, axis, axis=0)
        return [whole[at : at + most] for at in range(0, size, most)]
    found = [
        lax.ppermute(value, axis, [(i, i ^ (2 * k)) for i in range(size)]) for k in range(1, size // 2)
    ]
    own, _ = lax.optimization_barrier((value, ready))
    mine = jnp.stack([own] + found)
    return [mine, lax.ppermute(mine, axis, [(i, i ^ 1) for i in range(size)])]


def body(
    timeline, pointing, plate_angle, detector_angle, detector_weight, kernel, tile_owner, tile_block, wiener
):
    samples, dets = timeline.shape
    tiles = tile_owner.shape[0]
    devices = lax.axis_size("tm")
    partner, outside = neighbours(timeline, "tm")
    count_taps = kernel.shape[0]
    reach = (count_taps - 1) // 2
    width = count_taps - 1 + LANES
    pieces = [
        jnp.pad(kernel.astype(F32), (0, width - count_taps)), plate_angle, detector_angle, detector_weight,
        tile_owner.reshape(tiles).astype(F32), tile_block.reshape(tiles).astype(F32),
    ]
    used = sum(piece.shape[0] for piece in pieces)
    small = jnp.pad(jnp.concatenate(pieces), (0, -used % (8 * LANES))).reshape(-1, LANES)
    rows_own = ROWS // devices
    col_blocks = COLS // LANES
    vmem, hbm = pl.BlockSpec(memory_space=pltpu.VMEM), pl.BlockSpec(memory_space=pltpu.HBM)
    scalar = pl.BlockSpec(memory_space=pltpu.SMEM)
    place = lax.axis_index("tm").astype(jnp.int32).reshape(1)
    prepared = pl.pallas_call(
        functools.partial(prepare_kernel, rows_own, col_blocks, tiles),
        out_specs=[vmem] * 6,
        out_shape=[
            pltpu.VMEM((LANES, width), BF16),
            pltpu.VMEM((3, samples, dets), F32),
            pltpu.VMEM((samples, dets), jnp.int32),
            pltpu.VMEM((tiles // GROUP, GROUP * LOW, PIECE * LANES), BF16),
            pltpu.VMEM((samples, dets), BF16),
            pltpu.VMEM((8, 3 * LANES), F32),
        ],
        scratch_shapes=[pltpu.VMEM((samples, dets), jnp.int32)],
        compiler_params=pltpu.CompilerParams(vmem_limit_bytes=32 * 2**20),
        cost_estimate=pl.CostEstimate(flops=0, bytes_accessed=2**23, transcendentals=0),
        name="prepare",
    )(pointing, timeline, small)
    packed = pl.pallas_call(
        functools.partial(bin_kernel, reach),
        in_specs=[scalar] + [vmem] * 8,
        out_shape=jax.ShapeDtypeStruct((tiles + 8, 3 * LANES), F32),
        scratch_shapes=[
            pltpu.VMEM((2 * reach + samples, dets), BF16),
            pltpu.VMEM((3, samples, dets), F32),
            pltpu.VMEM((3 * GROUP * HIGH, PIECE * LANES), BF16),
        ],
        compiler_params=pltpu.CompilerParams(vmem_limit_bytes=40 * 2**20),
        name="bin_tiles",
    )(place, partner, outside, *[pltpu.with_memory_space_constraint(v, pltpu.VMEM) for v in prepared])
    stokes, count, ky = wiener.shape
    held, turns = pl.pallas_call(
        table_kernel,
        in_specs=[scalar, hbm, pl.BlockSpec(memory_space=pl.ANY)],
        out_specs=[vmem, vmem],
        out_shape=[pltpu.VMEM(wiener.shape, F32), pltpu.VMEM((2, count, 2 * LANES), BF16)],
        scratch_shapes=[pltpu.SemaphoreType.DMA],
        compiler_params=pltpu.CompilerParams(vmem_limit_bytes=4 * 2**20),
        cost_estimate=pl.CostEstimate(flops=0, bytes_accessed=2 * wiener.size * 4, transcendentals=0),
        name="tables",
    )(place, wiener, packed)
    in_vmem = functools.partial(pltpu.with_memory_space_constraint, memory_space=pltpu.VMEM)
    stacks = gather(packed, turns, "tm")
    held, turns = in_vmem(held), in_vmem(turns)
    early = len(stacks) == 2
    block = min(256, count)
    repeat = min(COLS // LANES, block)
    every = stacks[0].shape[0] // 2 * LANES
    lists = [pltpu.VMEM((every, 3 * LANES), F32), pltpu.VMEM((2, repeat, every), F32)]
    more = []
    if early:
        more = pl.pallas_call(
            functools.partial(early_kernel, block),
            in_specs=[scalar, vmem, vmem],
            out_specs=[vmem, vmem],
            scratch_shapes=lists,
            out_shape=[pltpu.VMEM((stokes, 2 * count, every), BF16), pltpu.VMEM((every, ky), BF16)],
            compiler_params=pltpu.CompilerParams(vmem_limit_bytes=12 * 2**20),
            cost_estimate=pl.CostEstimate(
                flops=12 * stokes * count * every * LANES, bytes_accessed=2**22, transcendentals=0
            ),
            name="early_factors",
        )(place, stacks.pop(0), turns)
        more = [in_vmem(v) for v in more]
    columns = every * (1 + early)
    spectra = pl.pallas_call(
        functools.partial(spectrum_kernel, early),
        in_specs=[scalar] + [vmem] * (3 + len(more)),
        out_specs=hbm,
        scratch_shapes=[
            lists[0],
            pltpu.VMEM((2 * block, columns), BF16),
            pltpu.VMEM((columns, ky), BF16),
            lists[1],
            pltpu.VMEM((2, 2, block, ky), F32),
            pltpu.SemaphoreType.DMA((2, 2, 3)),
        ],
        out_shape=jax.ShapeDtypeStruct((2, stokes, count, ky), F32),
        compiler_params=pltpu.CompilerParams(vmem_limit_bytes=40 * 2**20),
        name="spectra",
    )
    return sum(spectra(place, stack, held, turns, *more) for stack in stacks)


def solution(mesh):
    placed = (
        P("tm", "band"), P("tm", "band"), P("tm"), P("band"), P("band"), P("band"),
        P("tm", "band"), P("tm", "band"), P("band", "tm", None),
    )
    return jax.shard_map(
        body, mesh=mesh, in_specs=placed, out_specs=P(None, "band", "tm", None), check_vma=False
    )
```

```python
import functools
import math

import jax
import jax.numpy as jnp
from jax import lax
from jax.experimental import pallas as pl
from jax.experimental.pallas import tpu as pltpu
from jax.sharding import PartitionSpec as P

PIECE = 16
LANES = 128
LOW = 16
HIGH = LANES // LOW
ROWS = 2048
COLS = 4096
SCALE = 1.0 / math.sqrt(ROWS * COLS)
GROUP = 16
F32 = jnp.float32
BF16 = jnp.bfloat16
NT = (((1,), (1,)), ((), ()))


def iota(shape, dim):
    return lax.broadcasted_iota(jnp.int32, shape, dim)


def turn(m, modulus):
    quarter = modulus // 4
    quadrant = (m + quarter // 2) // quarter if quarter & (quarter - 1) else (
        lax.shift_right_logical(m + quarter // 2, int(math.log2(quarter))))
    x = (m - quadrant * quarter).astype(F32) * (2.0 * math.pi / modulus)
    y = x * x
    s = x + x * y * (-1.0 / 6 + y * (1.0 / 120 + y * (-1.0 / 5040 + y * (1.0 / 362880))))
    c = 1.0 + y * (-0.5 + y * (1.0 / 24 + y * (-1.0 / 720 + y * (1.0 / 40320))))
    swap = (quadrant & 1) == 1
    cos = jnp.where(swap, s, c)
    sin = jnp.where(swap, c, s)
    cos = jnp.where(((quadrant + 1) & 2) == 2, -cos, cos)
    sin = jnp.where((quadrant & 2) == 2, -sin, sin)
    return cos, sin


def halves(value):
    high = value.astype(BF16)
    return high, (value - high.astype(F32)).astype(BF16)


def column(row):
    return jnp.transpose(jnp.broadcast_to(row, (LANES, LANES)))


def prepare_kernel(
    rows_own, col_blocks,
    pixel_ref, time_ref, kernel_ref, plate_ref, angle_ref, weight_ref, owner_ref, block_ref,
    band_ref, factor_ref, high_ref, right_ref, own_ref, index_ref,
    low_ref, padded,
):
    samples, dets = pixel_ref.shape
    groups = dets // LANES
    pieces = GROUP // groups
    width = band_ref.shape[1]
    own_ref[...] = time_ref[...]
    count = kernel_ref.shape[1]
    padded[...] = jnp.zeros_like(padded)
    padded[:, :count] = kernel_ref[...].astype(F32)
    band_ref[...] = pltpu.roll(
        jnp.broadcast_to(padded[...], (LANES, width)), 0, axis=1, stride=1, stride_axis=0
    ).astype(BF16)
    angle, weight = angle_ref[...], weight_ref[...]
    cos_det, sin_det = jnp.cos(2.0 * angle) * weight, jnp.sin(2.0 * angle) * weight
    quad = 4.0 * plate_ref[...]
    cos_plate, sin_plate = jnp.cos(quad), jnp.sin(quad)
    for part in range(samples // LANES):
        span = slice(part * LANES, (part + 1) * LANES)
        cos_p = jnp.concatenate([column(cos_plate[part : part + 1])] * groups, axis=1)
        sin_p = jnp.concatenate([column(sin_plate[part : part + 1])] * groups, axis=1)
        factor_ref[0, span] = jnp.broadcast_to(weight, (LANES, dets))
        factor_ref[1, span] = cos_p * cos_det - sin_p * sin_det
        factor_ref[2, span] = sin_p * cos_det + cos_p * sin_det
    owner, block = owner_ref[...], block_ref[...]
    tiles = owner.shape[1]
    shift = int(math.log2(col_blocks))
    map_row = owner * rows_own + lax.shift_right_logical(block, shift)
    map_col = block & (col_blocks - 1)
    index_ref[...] = jnp.zeros_like(index_ref)
    for k, index in ((0, map_row), (1, map_col)):
        index_ref[k : k + 1, : 2 * tiles] = jnp.concatenate([index, index], axis=1).astype(F32)
    pixels = pixel_ref[...]
    high_ref[...] = lax.shift_right_logical(pixels, int(math.log2(LOW)))
    low_ref[...] = pixels & (LOW - 1)
    low_ids = iota((LOW, dets), 0)

    def piece_step(q, carry):
        g, p = lax.div(q, pieces), lax.rem(q, pieces)
        for t in range(PIECE):
            lanes = slice(t * LANES, (t + 1) * LANES)
            row = pl.ds(q * PIECE + t, 1)
            low = jnp.where(
                jnp.broadcast_to(low_ref[row, :], (LOW, dets)) == low_ids, 1.0, 0.0
            ).astype(BF16)
            for k in range(groups):
                at = pl.multiple_of((p * groups + k) * LOW, LOW)
                right_ref[g, pl.ds(at, LOW), lanes] = low[:, k * LANES : (k + 1) * LANES]
        return carry

    lax.fori_loop(0, samples // PIECE, piece_step, 0)


def bin_kernel(
    reach,
    place_ref, partner_ref, outside_ref, band_ref, factor_ref, high_ref, right_ref, own_ref, index_ref,
    out_ref,
    window, stokes, left_even, left_odd,
):
    samples, dets = own_ref.shape
    groups = dets // LANES
    is_first = lax.rem(place_ref[0], 2) == 0
    window[reach : reach + samples] = own_ref[...]

    @pl.when(is_first)
    def _():
        window[:reach] = outside_ref[samples - reach :]
        window[reach + samples :] = partner_ref[:reach]

    @pl.when(jnp.logical_not(is_first))
    def _():
        window[:reach] = partner_ref[samples - reach :]
        window[reach + samples :] = outside_ref[:reach]

    width = band_ref.shape[1]
    for part in range(samples // LANES):
        span = slice(part * LANES, (part + 1) * LANES)
        filtered = jnp.dot(
            band_ref[...], window[part * LANES : part * LANES + width, :], preferred_element_type=F32
        )
        for s in range(3):
            stokes[s, span] = (filtered * factor_ref[s, span]).astype(BF16).astype(F32)
    high_ids = iota((HIGH, dets), 0)
    pieces = GROUP // groups
    mine = lax.div(iota((HIGH, LANES), 1), LOW) == iota((HIGH, LANES), 0)
    stack = GROUP * HIGH
    tiles = (out_ref.shape[0] - index_ref.shape[0]) // 3

    def build(g, left):
        for p in range(pieces):
            for t in range(PIECE):
                k = (g * pieces + p) * PIECE + t
                row, lanes = slice(k, k + 1), slice(t * LANES, (t + 1) * LANES)
                hot = jnp.broadcast_to(high_ref[row, :], (HIGH, dets)) == high_ids
                for s in range(3):
                    spread = jnp.where(hot, jnp.broadcast_to(stokes[s, row, :], (HIGH, dets)), 0.0)
                    both = jnp.concatenate(
                        [spread[:, j * LANES : (j + 1) * LANES] for j in range(groups)], axis=0
                    )
                    at = s * stack + p * groups * HIGH
                    left[at : at + groups * HIGH, lanes] = both.astype(BF16)

    def collect(g, left):
        sums = lax.dot_general(left[...], right_ref[g], NT, preferred_element_type=F32)
        for s in range(3):
            rows = []
            for i in range(GROUP):
                start = (i * LOW) // LANES * LANES
                part = sums[s * stack + i * HIGH : s * stack + (i + 1) * HIGH, start : start + LANES]
                if start != i * LOW:
                    part = pltpu.roll(part, (start - i * LOW) % LANES, axis=1)
                part = pltpu.roll(part, 0, axis=1, stride=LOW, stride_axis=0)
                rows.append(jnp.sum(jnp.where(mine, part, 0.0), axis=0, keepdims=True))
            at = s * tiles + g * GROUP
            out_ref[at : at + GROUP] = jnp.concatenate(rows, axis=0)

    lefts = (left_even, left_odd)
    build(0, lefts[0])
    for g in range(tiles // GROUP):
        if (g + 1) * GROUP < tiles:
            build(g + 1, lefts[(g + 1) % 2])
        collect(g, lefts[g % 2])
    out_ref[3 * tiles :] = index_ref[...]


def table_kernel(place_ref, wiener_ref, ready_ref, held_ref, turns_ref, sem):
    del ready_ref
    copy = pltpu.make_async_copy(wiener_ref, held_ref, sem)
    copy.start()
    count = turns_ref.shape[1]
    first = place_ref[0] * count
    for at in range(0, count, LANES):
        size = min(LANES, count - at)
        kx = first + at + iota((size, LANES), 0)
        c, s = turn((kx * iota((size, LANES), 1)) & (COLS - 1), COLS)
        for k, value in enumerate((c * SCALE, s * -SCALE)):
            high, low = halves(value)
            turns_ref[k, at : at + size, :LANES] = high
            turns_ref[k, at : at + size, LANES:] = low
    copy.wait()


def expand(first, stack_ref, tiles, phases, table, start):
    parts = stack_ref.shape[0] // 2
    held = LANES // 2
    repeat = phases.shape[1]
    ky = table.shape[1]
    left_side = iota((1, LANES), 1) < held
    half_turns = 2 * ROWS - 1

    def build(p, carry):
        rows = pl.ds(pl.multiple_of(p * LANES, LANES), LANES)
        low, high = stack_ref.at[2 * p], stack_ref.at[2 * p + 1]
        for s in range(3):
            channel, some = slice(s * LANES, (s + 1) * LANES), slice(s * held, (s + 1) * held)
            tiles[pl.ds(pl.multiple_of(p * LANES, LANES), held), channel] = low[some]
            tiles[pl.ds(pl.multiple_of(p * LANES + held, held), held), channel] = high[some]
        at = 3 * held
        r = jnp.where(left_side, low[at : at + 1], high[at : at + 1])
        b = jnp.where(left_side, low[at + 1 : at + 2], high[at + 1 : at + 2])
        kx = first + iota((repeat, LANES), 0)
        c, s = turn((r.astype(jnp.int32) - kx * b.astype(jnp.int32) * LANES) & half_turns, 2 * ROWS)
        phases[0, :, rows] = c
        phases[1, :, rows] = s
        down = column(r).astype(jnp.int32)
        c, s = turn((r.astype(jnp.int32) * (2 * LANES)) & half_turns, 2 * ROWS)
        turn_c, turn_s = column(c), column(s)
        for g in range(0, LANES, 16):
            some = slice(g, g + 16)
            c, s = turn((down[some] * (2 * iota((16, LANES), 1) + 1)) & half_turns, 2 * ROWS)
            cs, ss = turn_c[some], turn_s[some]
            at = pl.ds(pl.multiple_of(start + p * LANES + g, 16), 16)
            for n in range(0, ky, 2 * LANES):
                table[at, n : n + LANES] = c.astype(BF16)
                table[at, n + LANES : n + 2 * LANES] = s.astype(BF16)
                c, s = c * cs - s * ss, c * ss + s * cs
        return carry

    lax.fori_loop(0, parts, build, 0, unroll=parts <= 4)


def factors(tiles, phases, turns_ref, rows, channel, at, size):
    high, low = halves(tiles[rows, channel])
    twice = jnp.concatenate([high, high], axis=1)
    real, imag = [
        lax.dot_general(turns_ref[side, at], twice, NT, preferred_element_type=F32)
        + lax.dot_general(turns_ref[side, at, :LANES], low, NT, preferred_element_type=F32)
        for side in range(2)
    ]
    pc = jnp.concatenate([phases[0, :, rows]] * (size // phases.shape[1]), axis=0)
    ps = jnp.concatenate([phases[1, :, rows]] * (size // phases.shape[1]), axis=0)
    return (real * pc - imag * ps).astype(BF16), (real * ps + imag * pc).astype(BF16)


def early_kernel(block, place_ref, stack_ref, turns_ref, factor_ref, table_ref, tiles, phases):
    stokes, count = factor_ref.shape[0], factor_ref.shape[1] // 2
    expand(place_ref[0] * count, stack_ref, tiles, phases, table_ref, 0)
    for s in range(stokes):
        channel = slice(s * LANES, (s + 1) * LANES)
        for k in range(0, count, block):
            real, imag = factors(
                tiles, phases, turns_ref, slice(None), channel, slice(k, k + block), block
            )
            factor_ref[s, k : k + block] = real
            factor_ref[s, count + k : count + k + block] = imag


def spectrum_kernel(early, place_ref, stack_ref, wiener_ref, turns_ref, *refs):
    ready_factor, ready_table = refs[:2] if early else (None, None)
    out_ref, tiles, factor, table, phases, buffer, sems = refs[2 * early :]
    stokes, count, ky = wiener_ref.shape
    block = factor.shape[0] // 2
    own = tiles.shape[0]
    ready = table.shape[0] - own
    if early:
        table[:ready] = ready_table[...]
    expand(place_ref[0] * count, stack_ref, tiles, phases, table, ready)
    half = ky // 2
    width = min(4 * LANES, own)
    flip = LANES - 1 - iota((block, LANES), 1)

    quarter = half // 2
    spans = ((0, quarter), (ky - quarter, quarter), (quarter, half))

    def copies(i, slot, which):
        s, k = lax.div(i, count // block), lax.rem(i, count // block)
        at = pl.ds(pl.multiple_of(k * block, block), block)
        for j in which:
            lanes = pl.ds(*spans[j])
            for side in range(2):
                yield pltpu.make_async_copy(
                    buffer.at[slot, side, :, lanes], out_ref.at[side, s, at, lanes], sems.at[slot, side, j]
                )

    def step(i, carry):
        slot = lax.rem(i, 2)
        s, k = lax.div(i, count // block), lax.rem(i, count // block)
        at = pl.ds(pl.multiple_of(k * block, block), block)
        channel = pl.ds(pl.multiple_of(s * LANES, LANES), LANES)

        def make(q, inner):
            rows = pl.ds(pl.multiple_of(q * width, width), width)
            into = pl.ds(pl.multiple_of(ready + q * width, LANES), width)
            real, imag = factors(tiles, phases, turns_ref, rows, channel, at, block)
            factor[:block, into] = real
            factor[block:, into] = imag
            return inner

        lax.fori_loop(0, own // width, make, 0)
        if early:
            under = pl.ds(pl.multiple_of(count + k * block, block), block)
            factor[:block, :ready] = ready_factor[s, at]
            factor[block:, :ready] = ready_factor[s, under]

        @pl.when(i >= 2)
        def _():
            for copy in copies(i, slot, (0, 1, 2)):
                copy.wait()

        for n in range(half // LANES):
            lanes = slice(n * LANES, (n + 1) * LANES)
            back = slice(ky - (n + 1) * LANES, ky - n * LANES)
            both = jnp.dot(
                factor[...], table[:, 2 * n * LANES : 2 * (n + 1) * LANES], preferred_element_type=F32
            )
            re_even, re_odd = both[:block, :LANES], both[:block, LANES:]
            im_even, im_odd = both[block:, :LANES], both[block:, LANES:]
            weight = wiener_ref[s, at, lanes]
            buffer[slot, 0, :, lanes] = (re_even + im_odd) * weight
            buffer[slot, 1, :, lanes] = (im_even - re_odd) * weight
            weight = wiener_ref[s, at, back]
            buffer[slot, 0, :, back] = jnp.take_along_axis(re_even - im_odd, flip, axis=1) * weight
            buffer[slot, 1, :, back] = jnp.take_along_axis(im_even + re_odd, flip, axis=1) * weight
            if (n + 1) * LANES == quarter:
                for copy in copies(i, slot, (0, 1)):
                    copy.start()
        for copy in copies(i, slot, (2,)):
            copy.start()
        return carry

    steps = stokes * (count // block)
    lax.fori_loop(0, steps, step, 0)
    for i in (steps - 2, steps - 1):
        for copy in copies(i, i % 2, (0, 1, 2)):
            copy.wait()


def neighbours(value, axis):
    size = lax.axis_size(axis)
    outer = [(i, i + 1) for i in range(1, size - 1, 2)]
    outside = lax.ppermute(value, axis, outer + [(j, i) for i, j in outer])
    return lax.ppermute(value, axis, [(i, i ^ 1) for i in range(size)]), outside


def gather(value, ready, axis):
    size = lax.axis_size(axis)
    most = 32
    if size > 8:
        whole = lax.all_gather(value, axis, axis=0)
        return [whole[at : at + most] for at in range(0, size, most)]
    found = [
        lax.ppermute(value, axis, [(i, i ^ (2 * k)) for i in range(size)]) for k in range(1, size // 2)
    ]
    own, _ = lax.optimization_barrier((value, ready))
    mine = jnp.stack([own] + found)
    return [mine, lax.ppermute(mine, axis, [(i, i ^ 1) for i in range(size)])]


def body(
    timeline, pointing, plate_angle, detector_angle, detector_weight, kernel, tile_owner, tile_block, wiener
):
    samples, dets = timeline.shape
    tiles = tile_owner.shape[0]
    devices = lax.axis_size("tm")
    partner, outside = neighbours(timeline, "tm")
    count_taps = kernel.shape[0]
    reach = (count_taps - 1) // 2
    width = count_taps - 1 + LANES
    rows_own = ROWS // devices
    col_blocks = COLS // LANES
    vmem, hbm = pl.BlockSpec(memory_space=pltpu.VMEM), pl.BlockSpec(memory_space=pltpu.HBM)
    scalar = pl.BlockSpec(memory_space=pltpu.SMEM)
    place = lax.axis_index("tm").astype(jnp.int32).reshape(1)
    prepared = pl.pallas_call(
        functools.partial(prepare_kernel, rows_own, col_blocks),
        out_specs=[vmem] * 6,
        out_shape=[
            pltpu.VMEM((LANES, width), BF16),
            pltpu.VMEM((3, samples, dets), F32),
            pltpu.VMEM((samples, dets), jnp.int32),
            pltpu.VMEM((tiles // GROUP, GROUP * LOW, PIECE * LANES), BF16),
            pltpu.VMEM((samples, dets), BF16),
            pltpu.VMEM((8, LANES), F32),
        ],
        scratch_shapes=[pltpu.VMEM((samples, dets), jnp.int32), pltpu.VMEM((1, width), F32)],
        compiler_params=pltpu.CompilerParams(vmem_limit_bytes=56 * 2**20),
        cost_estimate=pl.CostEstimate(flops=0, bytes_accessed=2**23, transcendentals=0),
        name="prepare",
    )(
        pointing, timeline, kernel.reshape(1, count_taps), plate_angle.reshape(samples // LANES, LANES),
        detector_angle.reshape(1, dets), detector_weight.reshape(1, dets),
        tile_owner.reshape(1, tiles), tile_block.reshape(1, tiles),
    )
    packed = pl.pallas_call(
        functools.partial(bin_kernel, reach),
        in_specs=[scalar] + [vmem] * 8,
        out_shape=jax.ShapeDtypeStruct((3 * tiles + 8, LANES), F32),
        scratch_shapes=[
            pltpu.VMEM((2 * reach + samples, dets), BF16),
            pltpu.VMEM((3, samples, dets), F32),
            pltpu.VMEM((3 * GROUP * HIGH, PIECE * LANES), BF16),
            pltpu.VMEM((3 * GROUP * HIGH, PIECE * LANES), BF16),
        ],
        compiler_params=pltpu.CompilerParams(vmem_limit_bytes=16 * 2**20),
        name="bin_tiles",
    )(place, partner, outside, *[pltpu.with_memory_space_constraint(v, pltpu.VMEM) for v in prepared])
    stokes, count, ky = wiener.shape
    held, turns = pl.pallas_call(
        table_kernel,
        in_specs=[scalar, hbm, pl.BlockSpec(memory_space=pl.ANY)],
        out_specs=[vmem, vmem],
        out_shape=[pltpu.VMEM(wiener.shape, F32), pltpu.VMEM((2, count, 2 * LANES), BF16)],
        scratch_shapes=[pltpu.SemaphoreType.DMA],
        compiler_params=pltpu.CompilerParams(vmem_limit_bytes=4 * 2**20),
        cost_estimate=pl.CostEstimate(flops=0, bytes_accessed=2 * wiener.size * 4, transcendentals=0),
        name="tables",
    )(place, wiener, packed)
    in_vmem = functools.partial(pltpu.with_memory_space_constraint, memory_space=pltpu.VMEM)
    stacks = gather(packed, turns, "tm")
    held, turns = in_vmem(held), in_vmem(turns)
    early = len(stacks) == 2
    block = min(256, count)
    repeat = min(COLS // LANES, block)
    every = stacks[0].shape[0] // 2 * LANES
    lists = [pltpu.VMEM((every, 3 * LANES), F32), pltpu.VMEM((2, repeat, every), F32)]
    more = []
    if early:
        more = pl.pallas_call(
            functools.partial(early_kernel, block),
            in_specs=[scalar, vmem, vmem],
            out_specs=[vmem, vmem],
            scratch_shapes=lists,
            out_shape=[pltpu.VMEM((stokes, 2 * count, every), BF16), pltpu.VMEM((every, ky), BF16)],
            compiler_params=pltpu.CompilerParams(vmem_limit_bytes=12 * 2**20),
            cost_estimate=pl.CostEstimate(
                flops=12 * stokes * count * every * LANES, bytes_accessed=2**22, transcendentals=0
            ),
            name="early_factors",
        )(place, stacks.pop(0), turns)
        more = [in_vmem(v) for v in more]
    columns = every * (1 + early)
    spectra = pl.pallas_call(
        functools.partial(spectrum_kernel, early),
        in_specs=[scalar] + [vmem] * (3 + len(more)),
        out_specs=hbm,
        scratch_shapes=[
            lists[0],
            pltpu.VMEM((2 * block, columns), BF16),
            pltpu.VMEM((columns, ky), BF16),
            lists[1],
            pltpu.VMEM((2, 2, block, ky), F32),
            pltpu.SemaphoreType.DMA((2, 2, 3)),
        ],
        out_shape=jax.ShapeDtypeStruct((2, stokes, count, ky), F32),
        compiler_params=pltpu.CompilerParams(vmem_limit_bytes=16 * 2**20),
        name="spectra",
    )
    return sum(spectra(place, stack, held, turns, *more) for stack in stacks)


def solution(mesh):
    placed = (
        P("tm", "band"), P("tm", "band"), P("tm"), P("band"), P("band"), P("band"),
        P("tm", "band"), P("tm", "band"), P("band", "tm", None),
    )
    return jax.shard_map(
        body, mesh=mesh, in_specs=placed, out_specs=P(None, "band", "tm", None), check_vma=False
    )
```

```python
import functools
import math

import jax
import jax.numpy as jnp
from jax import lax
from jax.experimental import pallas as pl
from jax.experimental.pallas import tpu as pltpu
from jax.sharding import PartitionSpec as P

PIECE = 16
LANES = 128
LOW = 16
HIGH = LANES // LOW
ROWS = 2048
COLS = 4096
SCALE = 1.0 / math.sqrt(ROWS * COLS)
GROUP = 16
F32 = jnp.float32
BF16 = jnp.bfloat16
NT = (((1,), (1,)), ((), ()))


def iota(shape, dim):
    return lax.broadcasted_iota(jnp.int32, shape, dim)


def turn(m, modulus):
    quarter = modulus // 4
    quadrant = (m + quarter // 2) // quarter if quarter & (quarter - 1) else (
        lax.shift_right_logical(m + quarter // 2, int(math.log2(quarter))))
    x = (m - quadrant * quarter).astype(F32) * (2.0 * math.pi / modulus)
    y = x * x
    s = x + x * y * (-1.0 / 6 + y * (1.0 / 120 + y * (-1.0 / 5040 + y * (1.0 / 362880))))
    c = 1.0 + y * (-0.5 + y * (1.0 / 24 + y * (-1.0 / 720 + y * (1.0 / 40320))))
    swap = (quadrant & 1) == 1
    cos = jnp.where(swap, s, c)
    sin = jnp.where(swap, c, s)
    cos = jnp.where(((quadrant + 1) & 2) == 2, -cos, cos)
    sin = jnp.where((quadrant & 2) == 2, -sin, sin)
    return cos, sin


def halves(value):
    high = value.astype(BF16)
    return high, (value - high.astype(F32)).astype(BF16)


def column(row):
    return jnp.transpose(jnp.broadcast_to(row, (LANES, LANES)))


def prepare_kernel(
    rows_own, col_blocks,
    pixel_ref, time_ref, kernel_ref, plate_ref, angle_ref, weight_ref, owner_ref, block_ref,
    band_ref, factor_ref, high_ref, right_ref, own_ref, index_ref,
    low_ref, padded,
):
    samples, dets = pixel_ref.shape
    groups = dets // LANES
    pieces = GROUP // groups
    width = band_ref.shape[1]
    own_ref[...] = time_ref[...]
    count = kernel_ref.shape[1]
    padded[...] = jnp.zeros_like(padded)
    padded[:, :count] = kernel_ref[...].astype(F32)
    band_ref[...] = pltpu.roll(
        jnp.broadcast_to(padded[...], (LANES, width)), 0, axis=1, stride=1, stride_axis=0
    ).astype(BF16)
    angle, weight = angle_ref[...], weight_ref[...]
    cos_det, sin_det = jnp.cos(2.0 * angle) * weight, jnp.sin(2.0 * angle) * weight
    quad = 4.0 * plate_ref[...]
    cos_plate, sin_plate = jnp.cos(quad), jnp.sin(quad)
    for part in range(samples // LANES):
        span = slice(part * LANES, (part + 1) * LANES)
        cos_p = jnp.concatenate([column(cos_plate[part : part + 1])] * groups, axis=1)
        sin_p = jnp.concatenate([column(sin_plate[part : part + 1])] * groups, axis=1)
        factor_ref[0, span] = jnp.broadcast_to(weight, (LANES, dets))
        factor_ref[1, span] = cos_p * cos_det - sin_p * sin_det
        factor_ref[2, span] = sin_p * cos_det + cos_p * sin_det
    owner, block = owner_ref[...], block_ref[...]
    tiles = owner.shape[1]
    shift = int(math.log2(col_blocks))
    map_row = owner * rows_own + lax.shift_right_logical(block, shift)
    map_col = block & (col_blocks - 1)
    index_ref[...] = jnp.zeros_like(index_ref)
    for k, index in ((0, map_row), (1, map_col)):
        index_ref[k : k + 1, : 2 * tiles] = jnp.concatenate([index, index], axis=1).astype(F32)
    pixels = pixel_ref[...]
    high_ref[...] = lax.shift_right_logical(pixels, int(math.log2(LOW)))
    low_ref[...] = pixels & (LOW - 1)
    low_ids = iota((LOW, dets), 0)

    def piece_step(q, carry):
        g, p = lax.div(q, pieces), lax.rem(q, pieces)
        for t in range(PIECE):
            lanes = slice(t * LANES, (t + 1) * LANES)
            row = pl.ds(q * PIECE + t, 1)
            low = jnp.where(
                jnp.broadcast_to(low_ref[row, :], (LOW, dets)) == low_ids, 1.0, 0.0
            ).astype(BF16)
            for k in range(groups):
                at = pl.multiple_of((p * groups + k) * LOW, LOW)
                right_ref[g, pl.ds(at, LOW), lanes] = low[:, k * LANES : (k + 1) * LANES]
        return carry

    lax.fori_loop(0, samples // PIECE, piece_step, 0)


def bin_kernel(
    reach,
    place_ref, partner_ref, outside_ref, band_ref, factor_ref, high_ref, right_ref, own_ref, index_ref,
    out_ref,
    window, stokes, left_even, left_odd,
):
    samples, dets = own_ref.shape
    groups = dets // LANES
    is_first = lax.rem(place_ref[0], 2) == 0
    window[reach : reach + samples] = own_ref[...]

    @pl.when(is_first)
    def _():
        window[:reach] = outside_ref[samples - reach :]
        window[reach + samples :] = partner_ref[:reach]

    @pl.when(jnp.logical_not(is_first))
    def _():
        window[:reach] = partner_ref[samples - reach :]
        window[reach + samples :] = outside_ref[:reach]

    width = band_ref.shape[1]
    for part in range(samples // LANES):
        span = slice(part * LANES, (part + 1) * LANES)
        filtered = jnp.dot(
            band_ref[...], window[part * LANES : part * LANES + width, :], preferred_element_type=F32
        )
        for s in range(3):
            stokes[s, span] = (filtered * factor_ref[s, span]).astype(BF16).astype(F32)
    high_ids = iota((HIGH, dets), 0)
    pieces = GROUP // groups
    mine = lax.div(iota((HIGH, LANES), 1), LOW) == iota((HIGH, LANES), 0)
    stack = GROUP * HIGH
    tiles = (out_ref.shape[0] - index_ref.shape[0]) // 3

    def build(g, left):
        for p in range(pieces):
            for t in range(PIECE):
                k = (g * pieces + p) * PIECE + t
                row, lanes = slice(k, k + 1), slice(t * LANES, (t + 1) * LANES)
                hot = jnp.broadcast_to(high_ref[row, :], (HIGH, dets)) == high_ids
                for s in range(3):
                    spread = jnp.where(hot, jnp.broadcast_to(stokes[s, row, :], (HIGH, dets)), 0.0)
                    both = jnp.concatenate(
                        [spread[:, j * LANES : (j + 1) * LANES] for j in range(groups)], axis=0
                    )
                    at = s * stack + p * groups * HIGH
                    left[at : at + groups * HIGH, lanes] = both.astype(BF16)

    def collect(g, left):
        sums = lax.dot_general(left[...], right_ref[g], NT, preferred_element_type=F32)
        for s in range(3):
            rows = []
            for i in range(GROUP):
                start = (i * LOW) // LANES * LANES
                part = sums[s * stack + i * HIGH : s * stack + (i + 1) * HIGH, start : start + LANES]
                if start != i * LOW:
                    part = pltpu.roll(part, (start - i * LOW) % LANES, axis=1)
                part = pltpu.roll(part, 0, axis=1, stride=LOW, stride_axis=0)
                rows.append(jnp.sum(jnp.where(mine, part, 0.0), axis=0, keepdims=True))
            at = s * tiles + g * GROUP
            out_ref[at : at + GROUP] = jnp.concatenate(rows, axis=0)

    lefts = (left_even, left_odd)
    build(0, lefts[0])
    for g in range(tiles // GROUP):
        if (g + 1) * GROUP < tiles:
            build(g + 1, lefts[(g + 1) % 2])
        collect(g, lefts[g % 2])
    out_ref[3 * tiles :] = index_ref[...]


def table_kernel(place_ref, wiener_ref, ready_ref, held_ref, turns_ref, sem):
    del ready_ref
    copy = pltpu.make_async_copy(wiener_ref, held_ref, sem)
    copy.start()
    count = turns_ref.shape[1]
    first = place_ref[0] * count
    for at in range(0, count, LANES):
        size = min(LANES, count - at)
        kx = first + at + iota((size, LANES), 0)
        c, s = turn((kx * iota((size, LANES), 1)) & (COLS - 1), COLS)
        for k, value in enumerate((c * SCALE, s * -SCALE)):
            high, low = halves(value)
            turns_ref[k, at : at + size, :LANES] = high
            turns_ref[k, at : at + size, LANES:] = low
    copy.wait()


def expand(first, stack_ref, tiles, phases, table, start):
    parts = stack_ref.shape[0] // 2
    held = LANES // 2
    repeat = phases.shape[1]
    ky = table.shape[1]
    left_side = iota((1, LANES), 1) < held
    half_turns = 2 * ROWS - 1

    def build(p, carry):
        rows = pl.ds(pl.multiple_of(p * LANES, LANES), LANES)
        low, high = stack_ref.at[2 * p], stack_ref.at[2 * p + 1]
        for s in range(3):
            channel, some = slice(s * LANES, (s + 1) * LANES), slice(s * held, (s + 1) * held)
            tiles[pl.ds(pl.multiple_of(p * LANES, LANES), held), channel] = low[some]
            tiles[pl.ds(pl.multiple_of(p * LANES + held, held), held), channel] = high[some]
        at = 3 * held
        r = jnp.where(left_side, low[at : at + 1], high[at : at + 1])
        b = jnp.where(left_side, low[at + 1 : at + 2], high[at + 1 : at + 2])
        kx = first + iota((repeat, LANES), 0)
        c, s = turn((r.astype(jnp.int32) - kx * b.astype(jnp.int32) * LANES) & half_turns, 2 * ROWS)
        phases[0, :, rows] = c
        phases[1, :, rows] = s
        down = column(r).astype(jnp.int32)
        c, s = turn((r.astype(jnp.int32) * (2 * LANES)) & half_turns, 2 * ROWS)
        turn_c, turn_s = column(c), column(s)
        for g in range(0, LANES, 16):
            some = slice(g, g + 16)
            c, s = turn((down[some] * (2 * iota((16, LANES), 1) + 1)) & half_turns, 2 * ROWS)
            cs, ss = turn_c[some], turn_s[some]
            at = pl.ds(pl.multiple_of(start + p * LANES + g, 16), 16)
            for n in range(0, ky, 2 * LANES):
                table[at, n : n + LANES] = c.astype(BF16)
                table[at, n + LANES : n + 2 * LANES] = s.astype(BF16)
                c, s = c * cs - s * ss, c * ss + s * cs
        return carry

    lax.fori_loop(0, parts, build, 0, unroll=parts <= 4)


def factors(tiles, phases, turns_ref, rows, channel, at, size):
    high, low = halves(tiles[rows, channel])
    twice = jnp.concatenate([high, high], axis=1)
    real, imag = [
        lax.dot_general(turns_ref[side, at], twice, NT, preferred_element_type=F32)
        + lax.dot_general(turns_ref[side, at, :LANES], low, NT, preferred_element_type=F32)
        for side in range(2)
    ]
    pc = jnp.concatenate([phases[0, :, rows]] * (size // phases.shape[1]), axis=0)
    ps = jnp.concatenate([phases[1, :, rows]] * (size // phases.shape[1]), axis=0)
    return (real * pc - imag * ps).astype(BF16), (real * ps + imag * pc).astype(BF16)


def early_kernel(block, place_ref, stack_ref, turns_ref, factor_ref, table_ref, tiles, phases):
    stokes, count = factor_ref.shape[0], factor_ref.shape[1] // 2
    expand(place_ref[0] * count, stack_ref, tiles, phases, table_ref, 0)
    for s in range(stokes):
        channel = slice(s * LANES, (s + 1) * LANES)
        for k in range(0, count, block):
            real, imag = factors(
                tiles, phases, turns_ref, slice(None), channel, slice(k, k + block), block
            )
            factor_ref[s, k : k + block] = real
            factor_ref[s, count + k : count + k + block] = imag


def spectrum_kernel(early, place_ref, stack_ref, wiener_ref, turns_ref, *refs):
    ready_factor, ready_table = refs[:2] if early else (None, None)
    out_ref, tiles, factor, second, table, phases, buffer, sems = refs[2 * early :]
    stokes, count, ky = wiener_ref.shape
    block = factor.shape[0] // 2
    own = tiles.shape[0]
    ready = table.shape[0] - own
    if early:
        table[:ready] = ready_table[...]
    expand(place_ref[0] * count, stack_ref, tiles, phases, table, ready)
    half = ky // 2
    width = min(4 * LANES, own)
    flip = LANES - 1 - iota((block, LANES), 1)

    quarter = half // 2
    spans = ((0, quarter), (ky - quarter, quarter), (quarter, half))

    def copies(i, slot, which):
        s, k = lax.div(i, count // block), lax.rem(i, count // block)
        at = pl.ds(pl.multiple_of(k * block, block), block)
        for j in which:
            lanes = pl.ds(*spans[j])
            for side in range(2):
                yield pltpu.make_async_copy(
                    buffer.at[slot, side, :, lanes], out_ref.at[side, s, at, lanes], sems.at[slot, side, j]
                )

    def place_of(i):
        s, k = lax.div(i, count // block), lax.rem(i, count // block)
        return s, k, pl.ds(pl.multiple_of(k * block, block), block)

    def make(i, factor):
        s, k, at = place_of(i)
        channel = pl.ds(pl.multiple_of(s * LANES, LANES), LANES)

        def some(q, inner):
            rows = pl.ds(pl.multiple_of(q * width, width), width)
            into = pl.ds(pl.multiple_of(ready + q * width, LANES), width)
            real, imag = factors(tiles, phases, turns_ref, rows, channel, at, block)
            factor[:block, into] = real
            factor[block:, into] = imag
            return inner

        if own == width:
            some(0, 0)
        else:
            lax.fori_loop(0, own // width, some, 0)
        if early:
            under = pl.ds(pl.multiple_of(count + k * block, block), block)
            factor[:block, :ready] = ready_factor[s, at]
            factor[block:, :ready] = ready_factor[s, under]

    def step(i, slot, factor, later):
        s, k, at = place_of(i)

        @pl.when(i >= 2)
        def _():
            for copy in copies(i, slot, (0, 1, 2)):
                copy.wait()

        if later is not None:
            make(lax.rem(i + 1, steps), later)
        for n in range(half // LANES):
            lanes = slice(n * LANES, (n + 1) * LANES)
            back = slice(ky - (n + 1) * LANES, ky - n * LANES)
            both = jnp.dot(
                factor[...], table[:, 2 * n * LANES : 2 * (n + 1) * LANES], preferred_element_type=F32
            )
            re_even, re_odd = both[:block, :LANES], both[:block, LANES:]
            im_even, im_odd = both[block:, :LANES], both[block:, LANES:]
            weight = wiener_ref[s, at, lanes]
            buffer[slot, 0, :, lanes] = (re_even + im_odd) * weight
            buffer[slot, 1, :, lanes] = (im_even - re_odd) * weight
            weight = wiener_ref[s, at, back]
            buffer[slot, 0, :, back] = jnp.take_along_axis(re_even - im_odd, flip, axis=1) * weight
            buffer[slot, 1, :, back] = jnp.take_along_axis(im_even + re_odd, flip, axis=1) * weight
            if (n + 1) * LANES == quarter:
                for copy in copies(i, slot, (0, 1)):
                    copy.start()
        for copy in copies(i, slot, (2,)):
            copy.start()

    steps = stokes * (count // block)
    make(jnp.int32(0), factor)

    def pair(j, carry):
        step(2 * j, 0, factor, second)
        step(2 * j + 1, 1, second, factor)
        return carry

    lax.fori_loop(0, steps // 2, pair, 0)
    if steps % 2:
        step(jnp.int32(steps - 1), 0, factor, None)
    for i in (steps - 2, steps - 1):
        for copy in copies(i, i % 2, (0, 1, 2)):
            copy.wait()


def neighbours(value, axis):
    size = lax.axis_size(axis)
    outer = [(i, i + 1) for i in range(1, size - 1, 2)]
    outside = lax.ppermute(value, axis, outer + [(j, i) for i, j in outer])
    return lax.ppermute(value, axis, [(i, i ^ 1) for i in range(size)]), outside


def gather(value, ready, axis):
    size = lax.axis_size(axis)
    most = 32
    if size > 8:
        whole = lax.all_gather(value, axis, axis=0)
        return [whole[at : at + most] for at in range(0, size, most)]
    found = [
        lax.ppermute(value, axis, [(i, i ^ (2 * k)) for i in range(size)]) for k in range(1, size // 2)
    ]
    own, _ = lax.optimization_barrier((value, ready))
    mine = jnp.stack([own] + found)
    return [mine, lax.ppermute(mine, axis, [(i, i ^ 1) for i in range(size)])]


def body(
    timeline, pointing, plate_angle, detector_angle, detector_weight, kernel, tile_owner, tile_block, wiener
):
    samples, dets = timeline.shape
    tiles = tile_owner.shape[0]
    devices = lax.axis_size("tm")
    partner, outside = neighbours(timeline, "tm")
    count_taps = kernel.shape[0]
    reach = (count_taps - 1) // 2
    width = count_taps - 1 + LANES
    rows_own = ROWS // devices
    col_blocks = COLS // LANES
    vmem, hbm = pl.BlockSpec(memory_space=pltpu.VMEM), pl.BlockSpec(memory_space=pltpu.HBM)
    scalar = pl.BlockSpec(memory_space=pltpu.SMEM)
    place = lax.axis_index("tm").astype(jnp.int32).reshape(1)
    prepared = pl.pallas_call(
        functools.partial(prepare_kernel, rows_own, col_blocks),
        out_specs=[vmem] * 6,
        out_shape=[
            pltpu.VMEM((LANES, width), BF16),
            pltpu.VMEM((3, samples, dets), F32),
            pltpu.VMEM((samples, dets), jnp.int32),
            pltpu.VMEM((tiles // GROUP, GROUP * LOW, PIECE * LANES), BF16),
            pltpu.VMEM((samples, dets), BF16),
            pltpu.VMEM((8, LANES), F32),
        ],
        scratch_shapes=[pltpu.VMEM((samples, dets), jnp.int32), pltpu.VMEM((1, width), F32)],
        compiler_params=pltpu.CompilerParams(vmem_limit_bytes=56 * 2**20),
        cost_estimate=pl.CostEstimate(flops=0, bytes_accessed=2**23, transcendentals=0),
        name="prepare",
    )(
        pointing, timeline, kernel.reshape(1, count_taps), plate_angle.reshape(samples // LANES, LANES),
        detector_angle.reshape(1, dets), detector_weight.reshape(1, dets),
        tile_owner.reshape(1, tiles), tile_block.reshape(1, tiles),
    )
    packed = pl.pallas_call(
        functools.partial(bin_kernel, reach),
        in_specs=[scalar] + [vmem] * 8,
        out_shape=jax.ShapeDtypeStruct((3 * tiles + 8, LANES), F32),
        scratch_shapes=[
            pltpu.VMEM((2 * reach + samples, dets), BF16),
            pltpu.VMEM((3, samples, dets), F32),
            pltpu.VMEM((3 * GROUP * HIGH, PIECE * LANES), BF16),
            pltpu.VMEM((3 * GROUP * HIGH, PIECE * LANES), BF16),
        ],
        compiler_params=pltpu.CompilerParams(vmem_limit_bytes=16 * 2**20),
        name="bin_tiles",
    )(place, partner, outside, *[pltpu.with_memory_space_constraint(v, pltpu.VMEM) for v in prepared])
    stokes, count, ky = wiener.shape
    held, turns = pl.pallas_call(
        table_kernel,
        in_specs=[scalar, hbm, pl.BlockSpec(memory_space=pl.ANY)],
        out_specs=[vmem, vmem],
        out_shape=[pltpu.VMEM(wiener.shape, F32), pltpu.VMEM((2, count, 2 * LANES), BF16)],
        scratch_shapes=[pltpu.SemaphoreType.DMA],
        compiler_params=pltpu.CompilerParams(vmem_limit_bytes=4 * 2**20),
        cost_estimate=pl.CostEstimate(flops=0, bytes_accessed=2 * wiener.size * 4, transcendentals=0),
        name="tables",
    )(place, wiener, packed)
    in_vmem = functools.partial(pltpu.with_memory_space_constraint, memory_space=pltpu.VMEM)
    stacks = gather(packed, turns, "tm")
    held, turns = in_vmem(held), in_vmem(turns)
    early = len(stacks) == 2
    block = min(256, count)
    repeat = min(COLS // LANES, block)
    every = stacks[0].shape[0] // 2 * LANES
    lists = [pltpu.VMEM((every, 3 * LANES), F32), pltpu.VMEM((2, repeat, every), F32)]
    more = []
    if early:
        more = pl.pallas_call(
            functools.partial(early_kernel, block),
            in_specs=[scalar, vmem, vmem],
            out_specs=[vmem, vmem],
            scratch_shapes=lists,
            out_shape=[pltpu.VMEM((stokes, 2 * count, every), BF16), pltpu.VMEM((every, ky), BF16)],
            compiler_params=pltpu.CompilerParams(vmem_limit_bytes=12 * 2**20),
            cost_estimate=pl.CostEstimate(
                flops=12 * stokes * count * every * LANES, bytes_accessed=2**22, transcendentals=0
            ),
            name="early_factors",
        )(place, stacks.pop(0), turns)
        more = [in_vmem(v) for v in more]
    columns = every * (1 + early)
    spectra = pl.pallas_call(
        functools.partial(spectrum_kernel, early),
        in_specs=[scalar] + [vmem] * (3 + len(more)),
        out_specs=hbm,
        scratch_shapes=[
            lists[0],
            pltpu.VMEM((2 * block, columns), BF16),
            pltpu.VMEM((2 * block, columns), BF16),
            pltpu.VMEM((columns, ky), BF16),
            lists[1],
            pltpu.VMEM((2, 2, block, ky), F32),
            pltpu.SemaphoreType.DMA((2, 2, 3)),
        ],
        out_shape=jax.ShapeDtypeStruct((2, stokes, count, ky), F32),
        compiler_params=pltpu.CompilerParams(vmem_limit_bytes=16 * 2**20),
        name="spectra",
    )
    return sum(spectra(place, stack, held, turns, *more) for stack in stacks)


def solution(mesh):
    placed = (
        P("tm", "band"), P("tm", "band"), P("tm"), P("band"), P("band"), P("band"),
        P("tm", "band"), P("tm", "band"), P("band", "tm", None),
    )
    return jax.shard_map(
        body, mesh=mesh, in_specs=placed, out_specs=P(None, "band", "tm", None), check_vma=False
    )
```
